256 devices in a mesh: seq: 32 (over z, y), head: 8 (over x, core).
Axes of the slice: x: 4, y: 4, z: 8, core: 2. Of those that a mesh axis runs over, the one named last changes fastest.
Arguments:
- queries: bfloat16 [16384, 4096], P('seq', 'head'), may hold values from -16 to 16
- latents: bfloat16 [384, 64, 1280], P('seq'), may hold values from -6 to 6
- key_weight: bfloat16 [1280, 4096], P(None, 'head'), may hold values from -0.15625 to 0.15625
- value_weight: bfloat16 [1280, 4096], P(None, 'head'), may hold values from -0.15625 to 0.15625
- visible: int32 [32, 16], P('seq'), may hold values from -1 to 63, as said below
- outbound: int32 [32, 32, 2], P('seq'), may hold values from -1 to 11, as said below
- token_slot: int32 [16384], P('seq'), may hold values from -1 to 15, as said below
- grad_out: bfloat16 [16384, 4096], P('seq', 'head'), may hold values from -6 to 6
Outputs:
- attended: bfloat16 [16384, 4096], P('seq', 'head')
- grad_queries: bfloat16 [16384, 4096], P('seq', 'head')
- grad_latents: float32 [384, 64, 1280], P('seq', 'head')
- grad_key_weight: float32 [1280, 4096], P('seq', 'head')
- grad_value_weight: float32 [1280, 4096], P('seq', 'head')
The draws below stay inside these ranges and needn't reach their ends.
Inputs may be any that keep to these rules, and one draw needn't show every extreme that they name: `visible`: row c lists each image that the tokens of text block c attend to once, in order of first appearance, then -1. An entry p names place p % 2 among the images that index p // 2 of seq holds and sends to block c. Some row lists 16 images. outbound[o, c, s] is the index, among the 12 images held by index o of seq (image o * 12 + index), of the image at place s of its sends to text block c, and -1 exactly where no entry of row c of visible names that place. No block attends to more than 2 images of one holder, and some block attends to exactly 2 images of one holder. `token_slot`: documents are 8192 tokens long and start at multiples of 8192; the first 32 tokens of every document, and any others before its first image, have -1. Within a text block the slot never falls and changes only at positions that are multiples of 32, by one at a time.
All inputs are finite; a program needn't handle non-finite values.
Results may differ from the reference program's by a relative error of at most 0.012.
Values may be sent and summed in bfloat16 or wider, within the bound.
No kernel may reach another device: no remote copies, remote signals or barrier semaphores. Data moves between devices by JAX's collectives and lax.ppermute only.
A program may use at most 128 MiB of HBM per device.

```python
import jax
import jax.numpy as jnp
from jax import lax

DV = 1280
LAT = 64
DH = 128
H = 32
TOK_DEV = 512
GAP = 32
DOC = 8192
HD = 4096
TEXT_BLOCKS = 32
TOKENS = 16384
VIS = 16
IMG_DEV = 12
IMAGES = 384
SLOTS = 2


def image_for_event(event_ids, holder_perm):
    group_ids = event_ids // SLOTS
    holder = holder_perm[group_ids % TEXT_BLOCKS]
    local_ids = event_ids // (TEXT_BLOCKS * SLOTS) * SLOTS + event_ids % SLOTS
    return (holder, local_ids)


def build_layout(key):
    grid_size = TOK_DEV // GAP
    per_doc = DOC // TOK_DEV
    spread = VIS - 1 - IMG_DEV
    key_pair, key_amount, key_place, key_holder = jax.random.split(jax.random.fold_in(key, 7), 4)
    block_ids = jnp.arange(TEXT_BLOCKS, dtype=jnp.int32)
    doc_start = block_ids % per_doc == 0
    pair_score = jax.random.randint(key_pair, (TEXT_BLOCKS,), 0, 4096) * TEXT_BLOCKS + block_ids
    pair_score = pair_score + jnp.where(doc_start, 1 << 24, 0)
    pairing = jnp.argsort(pair_score).astype(jnp.int32)
    amounts = jax.random.randint(key_amount, (TEXT_BLOCKS // 2,), 0, spread + 1)
    amounts = amounts.at[0].set(spread)
    event_shift = jnp.zeros((TEXT_BLOCKS,), jnp.int32).at[pairing[0::2]].set(amounts).at[pairing[1::2]].set(-amounts)
    events = IMG_DEV + event_shift
    heavy = pairing[0]
    grid_ids = jnp.arange(grid_size, dtype=jnp.int32)
    place_score = jax.random.randint(key_place, (TEXT_BLOCKS, grid_size), 0, 4096) * grid_size + grid_ids[None, :]
    barred = ((block_ids[:, None] == heavy) | doc_start[:, None]) & (grid_ids[None, :] == 0)
    place_score = place_score + jnp.where(barred, 1 << 24, 0)
    place_rank = jnp.argsort(jnp.argsort(place_score, axis=1), axis=1)
    event_flags = (place_rank < events[:, None]).astype(jnp.int32).reshape(-1)
    count_upto = jnp.cumsum(event_flags)
    last_event = count_upto - 1
    groups_doc = DOC // GAP
    group_ids = jnp.arange(TEXT_BLOCKS * grid_size, dtype=jnp.int32)
    doc_first = group_ids // groups_doc * groups_doc
    before_doc = count_upto[doc_first] - event_flags[doc_first]
    seen_event = jnp.where(last_event >= before_doc, last_event, -1).reshape(TEXT_BLOCKS, grid_size)
    lowest = jnp.min(jnp.where(seen_event >= 0, seen_event, IMAGES), axis=1)
    highest = jnp.max(seen_event, axis=1)
    counts = highest - lowest + 1
    slot_groups = jnp.where(seen_event >= 0, seen_event - lowest[:, None], -1)
    token_slot = jnp.repeat(slot_groups.reshape(-1), GAP)
    holder_perm = jax.random.permutation(key_holder, TEXT_BLOCKS).astype(jnp.int32)
    first_group = (lowest[heavy] + SLOTS - 1) // SLOTS
    wanted = first_group % TEXT_BLOCKS
    current = jnp.argmax(holder_perm == TEXT_BLOCKS - 1).astype(jnp.int32)
    holder_perm = holder_perm.at[current].set(holder_perm[wanted]).at[wanted].set(TEXT_BLOCKS - 1)
    slot_ids = jnp.arange(VIS, dtype=jnp.int32)
    filled = slot_ids[None, :] < counts[:, None]
    event_ids = jnp.minimum(lowest[:, None] + slot_ids[None, :], IMAGES - 1)
    holder, local_ids = image_for_event(event_ids, holder_perm)
    earlier = (holder[:, :, None] == holder[:, None, :]) & filled[:, None, :] & (slot_ids[None, None, :] < slot_ids[None, :, None])
    ordinal = jnp.sum(earlier.astype(jnp.int32), axis=2)
    visible = jnp.where(filled, holder * SLOTS + ordinal, -1).astype(jnp.int32)
    rows_holder = jnp.where(filled, holder, TEXT_BLOCKS)
    column_blocks = jnp.broadcast_to(block_ids[:, None], rows_holder.shape)
    outbound = jnp.full((TEXT_BLOCKS, TEXT_BLOCKS, SLOTS), -1, jnp.int32)
    outbound = outbound.at[rows_holder, column_blocks, ordinal].set(local_ids.astype(jnp.int32), mode='drop')
    return (visible, outbound, token_slot.astype(jnp.int32))


def draw_visible(key, part):
    return build_layout(key)[0]


def draw_outbound(key, part):
    return build_layout(key)[1]


def draw_token_slot(key, part):
    return build_layout(key)[2]


def draw_queries(key, part):
    key_main = jax.random.fold_in(jax.random.fold_in(key, 11), 0)
    base_draw = jnp.clip(jax.random.normal(key_main, (TOKENS, HD), jnp.float32), -4.0, 4.0)
    return base_draw.astype(jnp.bfloat16)


def strengthened(result, own_key, source, target, blocks, factor):
    def block_of(axis_at):
        return (jnp.arange(result.shape[axis_at]) // (result.shape[axis_at] // blocks)).reshape((-1,) + (1,) * (result.ndim - 1 - axis_at))

    near = jax.random.permutation(own_key, blocks)[block_of(target)]
    other_side = (block_of(target) + blocks // 2) % blocks
    return jnp.where((block_of(source) == near) | (block_of(source) == other_side), factor * result, result)


def level_of(rng, shape, cuts, least, largest):
    factor_of = 1.0
    for axis_at, parts in cuts:
        draws = jax.random.uniform(jax.random.fold_in(jax.random.fold_in(rng, 6), axis_at), (parts,), jnp.float32, least / len(cuts), largest / len(cuts))
        factor_of = factor_of * jnp.repeat(jnp.exp(draws), shape[axis_at] // parts).reshape((-1,) + (1,) * (len(shape) - 1 - axis_at))
    return factor_of


def bell_draw(own_key, extent, width, bound, cuts=(), kind=jnp.bfloat16):
    array = width * jax.random.normal(own_key, extent, jnp.float32)
    if cuts:
        array = array * level_of(own_key, extent, cuts, -0.22, 0.18)
    return jnp.clip(array, -bound, bound).astype(kind)


def noise_with(key, dims, scale, bound, shards, heavy, held_as=jnp.bfloat16):
    values = scale * jax.random.normal(key, dims, jnp.float32)
    if shards:
        values = values * level_of(key, dims, shards, -0.22, 0.18)
    return jnp.clip(strengthened(values, jax.random.fold_in(key, 3), *heavy), -bound, bound).astype(held_as)


def setup_inputs(seed: int = 0) -> dict:
    seeds = jax.random.split(jax.random.key(seed), 9)
    return {
        "queries": draw_queries(jax.random.fold_in(seeds[8], 71), 0),
        "latents": noise_with(seeds[1], (IMAGES, LAT, DV), 1.0, 6.0, ((0, 32),), (0, 2, 32, 2.75)),
        "key_weight": bell_draw(seeds[2], (DV, HD), DV ** -0.5, 0.15625, ((1, 8),)),
        "value_weight": bell_draw(seeds[3], (DV, HD), DV ** -0.5, 0.15625, ((1, 8),)),
        "visible": draw_visible(jax.random.fold_in(seeds[8], 71), 0),
        "outbound": draw_outbound(jax.random.fold_in(seeds[8], 71), 0),
        "token_slot": draw_token_slot(jax.random.fold_in(seeds[8], 71), 0),
        "grad_out": bell_draw(seeds[7], (TOKENS, HD), 1.0, 6.0, ((0, 32), (1, 8))),
    }


def block_pass(packed, keys_all, values_all):
    query_part, grad_part, group_slot, image_ids = packed
    score_scale = DH ** -0.5
    present = group_slot >= 0
    group_image = image_ids[jnp.maximum(group_slot, 0)]
    key_group = keys_all[group_image].astype(jnp.float32)
    value_group = values_all[group_image].astype(jnp.float32)
    query_wide = query_part.astype(jnp.float32)
    scores = jnp.einsum("gthd,gjhd->gthj", query_wide, key_group, precision=lax.Precision.HIGHEST) * score_scale
    row_peak = jnp.max(scores, axis=-1, keepdims=True)
    exp_terms = jnp.exp(scores - row_peak)
    prob_full = exp_terms / jnp.sum(exp_terms, axis=-1, keepdims=True)
    prob_low = prob_full.astype(jnp.bfloat16)
    weight_mask = present[:, None, None, None]
    mixed_out = jnp.einsum("gthj,gjhd->gthd", prob_low.astype(jnp.float32), value_group, precision=lax.Precision.HIGHEST)
    attended = jnp.where(weight_mask, mixed_out, jnp.zeros_like(mixed_out)).astype(jnp.bfloat16)
    grad_masked = jnp.where(weight_mask, grad_part, jnp.zeros_like(grad_part))
    grad_wide = grad_masked.astype(jnp.float32)
    grad_prob = jnp.einsum("gthd,gjhd->gthj", grad_wide, value_group, precision=lax.Precision.HIGHEST)
    row_inner = jnp.sum(prob_full * grad_prob, axis=-1, keepdims=True)
    grad_score = (prob_full * (grad_prob - row_inner) * score_scale).astype(jnp.bfloat16)
    score_wide = grad_score.astype(jnp.float32)
    grad_query = jnp.einsum("gthj,gjhd->gthd", score_wide, key_group, precision=lax.Precision.HIGHEST).astype(jnp.bfloat16)
    key_term = jnp.einsum("gthj,gthd->gjhd", score_wide, query_wide, precision=lax.Precision.HIGHEST)
    value_term = jnp.einsum("gthj,gthd->gjhd", prob_low.astype(jnp.float32), grad_wide, precision=lax.Precision.HIGHEST)
    slot_match = (jnp.arange(VIS, dtype=jnp.int32)[:, None] == group_slot[None, :].astype(jnp.int32)).astype(jnp.float32)
    key_slot = jnp.einsum("vg,gjhd->vjhd", slot_match, key_term, precision=lax.Precision.HIGHEST).astype(jnp.bfloat16)
    value_slot = jnp.einsum("vg,gjhd->vjhd", slot_match, value_term, precision=lax.Precision.HIGHEST).astype(jnp.bfloat16)
    return attended, grad_query, key_slot, value_slot


def reference(queries, latents, key_weight, value_weight, visible, outbound, token_slot, grad_out):
    flat_lat = latents.reshape(IMAGES * LAT, DV)
    keys_all = jnp.dot(flat_lat, key_weight, preferred_element_type=jnp.float32).astype(jnp.bfloat16).reshape(IMAGES, LAT, H, DH)
    values_all = jnp.dot(flat_lat, value_weight, preferred_element_type=jnp.float32).astype(jnp.bfloat16).reshape(IMAGES, LAT, H, DH)
    groups_each = TOK_DEV // GAP
    holder_ids = (jnp.maximum(visible, 0) // SLOTS).astype(jnp.int32)
    ordinal_ids = (jnp.maximum(visible, 0) % SLOTS).astype(jnp.int32)
    block_ids = jnp.broadcast_to(jnp.arange(TEXT_BLOCKS, dtype=jnp.int32)[:, None], visible.shape)
    local_ids = outbound[holder_ids, block_ids, ordinal_ids]
    image_ids = jnp.where(visible >= 0, holder_ids * IMG_DEV + local_ids, 0).astype(jnp.int32)
    query_blocks = queries.reshape(TEXT_BLOCKS, groups_each, GAP, H, DH)
    grad_groups = grad_out.reshape(TEXT_BLOCKS, groups_each, GAP, H, DH)
    group_slots = token_slot.reshape(TEXT_BLOCKS, groups_each, GAP)[:, :, 0]

    def visit_block(packed):
        return block_pass(packed, keys_all, values_all)

    results = lax.map(visit_block, (query_blocks, grad_groups, group_slots, image_ids))
    attended = results[0].reshape(TOKENS, HD)
    grad_queries = results[1].reshape(TOKENS, HD)
    targets = jnp.where(visible >= 0, image_ids, IMAGES).astype(jnp.int32).reshape(-1)
    key_grad = jnp.zeros((IMAGES, LAT, H, DH), jnp.float32).at[targets].add(
        results[2].reshape(TEXT_BLOCKS * VIS, LAT, H, DH).astype(jnp.float32), mode="drop")
    value_grad = jnp.zeros((IMAGES, LAT, H, DH), jnp.float32).at[targets].add(
        results[3].reshape(TEXT_BLOCKS * VIS, LAT, H, DH).astype(jnp.float32), mode="drop")
    key_grad = key_grad.astype(jnp.bfloat16).reshape(IMAGES * LAT, HD)
    value_grad = value_grad.astype(jnp.bfloat16).reshape(IMAGES * LAT, HD)
    grad_latents = jnp.dot(key_grad, key_weight.T, preferred_element_type=jnp.float32)
    grad_latents = grad_latents + jnp.dot(value_grad, value_weight.T, preferred_element_type=jnp.float32)
    grad_latents = grad_latents.reshape(IMAGES, LAT, DV)
    grad_key_weight = jnp.dot(flat_lat.T, key_grad, preferred_element_type=jnp.float32)
    grad_value_weight = jnp.dot(flat_lat.T, value_grad, preferred_element_type=jnp.float32)
    return attended, grad_queries, grad_latents, grad_key_weight, grad_value_weight
```

```python
import jax
import jax.numpy as jnp
from jax import lax
from jax.experimental import pallas as pl
from jax.experimental.pallas import tpu as pltpu
from jax.sharding import Mesh
from jax.sharding import PartitionSpec as P

DH = 128
GAP = 32
WIN = 4
SUB = 8
NEG_FILL = -1e30
BF = jnp.bfloat16
F32 = jnp.float32

NN = (((1,), (0,)), ((), ()))
NT = (((1,), (1,)), ((), ()))
TN = (((0,), (0,)), ((), ()))


def mm(a, b, dims):
    return lax.dot_general(a, b, dims, preferred_element_type=F32)


def shift(v, axis, step, size):
    return lax.ppermute(v, axis, [(i, (i + step) % size) for i in range(size)])


def add2(a, b):
    return (a.astype(F32) + b.astype(F32)).astype(BF)


def vmem():
    return pl.BlockSpec(memory_space=pltpu.VMEM)


def smem():
    return pl.BlockSpec(memory_space=pltpu.SMEM)


def main_kernel(
    start_ref, mine_ref, other_ref, wk_ref, wv_ref, q_ref, g_ref, slot_ref,
    att_ref, dq_ref, bg_ref, lat_ref, dl_ref,
    k_ref, v_ref, acc_ref,
):
    vis = mine_ref.shape[1]
    rows = 2 * mine_ref.shape[0] * SUB
    width = mine_ref.shape[3]
    cols = wk_ref.shape[1]
    heads = cols // DH
    chunk = WIN * rows

    @pl.loop(0, vis // WIN)
    def _(i):
        mine = mine_ref[:, pl.ds(i * WIN, WIN)].astype(F32)
        other = other_ref[:, pl.ds(i * WIN, WIN)].astype(F32)
        parts = []
        for s in range(WIN):
            parts.append(mine[:, s].reshape(rows // 2, width))
            parts.append(other[:, s].reshape(rows // 2, width))
        x = jnp.concatenate(parts, axis=0).astype(BF)
        at = pl.ds(pl.multiple_of(i * chunk, chunk), chunk)
        lat_ref[at, :] = x
        k_ref[at, :] = mm(x, wk_ref[...], NN).astype(BF)
        v_ref[at, :] = mm(x, wv_ref[...], NN).astype(BF)
        acc_ref[at, :] = jnp.zeros((chunk, 2 * cols), F32)

    span = WIN * GAP
    scale = DH ** (-0.5)

    @pl.loop(0, q_ref.shape[0] // span)
    def _(w):
        first = start_ref[w]
        at = pl.ds(pl.multiple_of(first * rows, rows), chunk)
        tok = pl.ds(pl.multiple_of(w * span, span), span)
        slot = slot_ref[w]
        key_slot = first + lax.broadcasted_iota(jnp.int32, (chunk, span), 0) // rows
        match = key_slot == slot
        for h in range(heads):
            c = slice(h * DH, (h + 1) * DH)
            q = q_ref[tok, c]
            g = g_ref[tok, c]
            k = k_ref[at, c]
            v = v_ref[at, c]
            s = jnp.where(match, mm(k, q, NT) * scale, NEG_FILL)
            e = jnp.where(match, jnp.exp(s - jnp.max(s, axis=0, keepdims=True)), 0.0)
            total = jnp.sum(e, axis=0, keepdims=True)
            p = e / jnp.where(total > 0.0, total, 1.0)
            pb = p.astype(BF)
            att_ref[tok, c] = mm(pb, v, TN).astype(BF)
            dp = mm(v, g, NT)
            inner = jnp.sum(p * dp, axis=0, keepdims=True)
            ds = (p * (dp - inner) * scale).astype(BF)
            dq_ref[tok, c] = mm(ds, k, TN).astype(BF)
            acc_ref[at, c] += mm(ds, q, NN)
            acc_ref[at, slice(cols + h * DH, cols + (h + 1) * DH)] += mm(pb, g, NN)

    @pl.loop(0, vis // WIN)
    def _(i):
        at = pl.ds(pl.multiple_of(i * chunk, chunk), chunk)
        grad = acc_ref[at, :].astype(BF)
        bg_ref[at, :] = grad
        out = mm(grad[:, :cols], wk_ref[...], NT) + mm(grad[:, cols:], wv_ref[...], NT)
        for s in range(WIN):
            piece = out[s * rows:(s + 1) * rows].reshape(rows // SUB, SUB, width)
            dl_ref[:, i * WIN + s] = piece.astype(BF)


def weight_kernel(y_ref, lat_ref, bg_ref, out_ref, t_ref):
    ny, nz, part, cols = out_ref.shape
    half = t_ref.shape[0]
    step = 256
    me = y_ref[0]
    for j in range(lat_ref.shape[1] // half):
        t_ref[...] = lat_ref[:, j * half:(j + 1) * half].T

        @pl.loop(0, cols // step)
        def _(n):
            at = pl.ds(pl.multiple_of(n * step, step), step)
            r = mm(t_ref[...], bg_ref[:, at], NN).astype(BF)
            for b in range(half // part):
                piece = j * (half // part) + b
                rel = lax.rem(piece % ny - me + ny, ny)
                out_ref[rel, piece // ny, :, at] = r[b * part:(b + 1) * part]


def collect_kernel(sent_ref, got_ref, out_ref):
    out_ref[...] = jnp.zeros_like(out_ref)

    @pl.loop(0, got_ref.shape[0])
    def _(e):
        image = sent_ref[e]

        @pl.when(image >= 0)
        def _():
            out_ref[image] += got_ref[e].astype(F32)


def local(queries, latents, key_weight, value_weight, visible, outbound, token_slot, grad_out):
    seq = ("z", "y")
    head = ("x", "core")
    nz, ny, nx = (lax.axis_size(a) for a in ("z", "y", "x"))
    tokens, cols = queries.shape
    images, lat_rows, width = latents.shape
    vis = visible.shape[1]
    sent = outbound[0].reshape(-1)
    places = visible[0]
    slots_total = sent.shape[0]
    row_groups = lat_rows // SUB
    part = width // (nz * ny)
    params = pltpu.CompilerParams(vmem_limit_bytes=56 * 1024 * 1024)

    me = lax.axis_index(head)
    pick = jnp.maximum(sent, 0) * row_groups + me
    send = latents.reshape(images * row_groups, SUB, width)[pick]
    got = lax.all_to_all(send, seq, split_axis=0, concat_axis=0, tiled=True)
    own = got[jnp.maximum(places, 0)]

    left = shift(own, "x", 1, nx)
    right = shift(own, "x", -1, nx)
    half = vis // 2
    far_a = shift(left[:half], "x", 1, nx)
    far_b = shift(right[half:], "x", -1, nx)
    mine = jnp.concatenate([own, left, right, far_a, far_b], axis=0).reshape(nx, vis, SUB, width)
    other = shift(mine, "core", 1, 2)

    span = WIN * GAP
    windows = tokens // span
    slot_rows = token_slot.reshape(windows, 1, span)
    start = jnp.minimum(jnp.maximum(slot_rows[:, 0, 0], 0), vis - WIN)
    keys = vis * lat_rows
    att, dq, bg, lat_all, dl = pl.pallas_call(
        main_kernel,
        name="main",
        out_shape=(
            jax.ShapeDtypeStruct((tokens, cols), BF),
            jax.ShapeDtypeStruct((tokens, cols), BF),
            jax.ShapeDtypeStruct((keys, 2 * cols), BF),
            jax.ShapeDtypeStruct((keys, width), BF),
            jax.ShapeDtypeStruct((row_groups, vis, SUB, width), BF),
        ),
        in_specs=[smem()] + [vmem()] * 7,
        out_specs=tuple([vmem()] * 5),
        scratch_shapes=[
            pltpu.VMEM((keys, cols), BF),
            pltpu.VMEM((keys, cols), BF),
            pltpu.VMEM((keys, 2 * cols), F32),
        ],
        compiler_params=params,
        cost_estimate=pl.CostEstimate(
            flops=8 * keys * width * cols + 16 * keys * span * cols,
            bytes_accessed=16 * 1024 * 1024,
            transcendentals=tokens * 4 * 256,
        ),
    )(start, mine, other, key_weight, value_weight, queries, grad_out, slot_rows)

    swapped = shift(dl[nx:], "core", 1, 2)
    summed = add2(dl[:nx], swapped)
    up = shift(summed[3, :half], "x", 1, nx)
    down = shift(summed[3, half:], "x", -1, nx)
    to_right = jnp.concatenate([add2(summed[2, :half], up), summed[2, half:]], axis=0)
    to_left = jnp.concatenate([summed[1, :half], add2(summed[1, half:], down)], axis=0)
    from_left = shift(to_right, "x", 1, nx)
    from_right = shift(to_left, "x", -1, nx)
    dl_mine = (summed[0].astype(F32) + from_left.astype(F32) + from_right.astype(F32)).astype(BF)

    y_here = lax.axis_index("y")
    gw = pl.pallas_call(
        weight_kernel,
        name="weights",
        out_shape=jax.ShapeDtypeStruct((ny, nz, part, 2 * cols), BF),
        in_specs=[smem(), vmem(), vmem()],
        out_specs=vmem(),
        scratch_shapes=[pltpu.VMEM((width // 2, keys), BF)],
        compiler_params=params,
        cost_estimate=pl.CostEstimate(
            flops=4 * keys * width * cols, bytes_accessed=8 * 1024 * 1024, transcendentals=0
        ),
    )(y_here.reshape(1).astype(jnp.int32), lat_all, bg)

    zh = nz // 2
    gw_up = shift(gw[2, :zh], "y", 1, ny)
    gw_down = shift(gw[2, zh:], "y", -1, ny)
    gw_next = jnp.concatenate([add2(gw[1, :zh], gw_up), gw[1, zh:]], axis=0)
    gw_prev = jnp.concatenate([gw[3, :zh], add2(gw[3, zh:], gw_down)], axis=0)
    gw_l = shift(gw_next, "y", 1, ny)
    gw_r = shift(gw_prev, "y", -1, ny)
    gw_y = (gw[0].astype(F32) + gw_l.astype(F32) + gw_r.astype(F32)).astype(BF)

    hits = places[None, :] == jnp.arange(slots_total, dtype=jnp.int32)[:, None]
    back = dl_mine[jnp.argmax(hits, axis=1)]
    returned = lax.all_to_all(back, seq, split_axis=0, concat_axis=0, tiled=True)

    z_here = lax.axis_index("z")
    weights = lax.dynamic_index_in_dim(gw_y, z_here, 0, False).astype(F32)
    for step in (1, -1, 2, -2, 3, -3, 4):
        piece = lax.dynamic_index_in_dim(gw_y, lax.rem(z_here + step + nz, nz), 0, False)
        weights = weights + shift(piece, "z", step, nz).astype(F32)

    grad_latents = pl.pallas_call(
        collect_kernel,
        name="collect",
        out_shape=jax.ShapeDtypeStruct((images, SUB, width), F32),
        in_specs=[smem(), vmem()],
        out_specs=vmem(),
        compiler_params=params,
    )(sent, returned)
    return att, dq, grad_latents, weights[:, :cols], weights[:, cols:]


def solution(mesh):
    sizes = mesh.shape
    nz, ny, nx, core = 8, 4, 4, 2
    assert (sizes["seq"], sizes["head"]) == (nz * ny, nx * core)
    grid = Mesh(mesh.devices.reshape(nz, ny, nx, core), ("z", "y", "x", "core"))
    seq = ("z", "y")
    head = ("x", "core")
    in_specs = (
        P(seq, head),
        P(seq, None, None),
        P(None, head),
        P(None, head),
        P(seq, None),
        P(seq, None, None),
        P(seq),
        P(seq, head),
    )
    out_specs = (
        P(seq, head),
        P(seq, head),
        P(seq, head, None),
        P(seq, head),
        P(seq, head),
    )
    return jax.shard_map(local, mesh=grid, in_specs=in_specs, out_specs=out_specs, check_vma=False)
```

```python
import jax
import jax.numpy as jnp
from jax import lax
from jax.experimental import pallas as pl
from jax.experimental.pallas import tpu as pltpu
from jax.sharding import Mesh
from jax.sharding import PartitionSpec as P

DH = 128
GAP = 32
WIN = 4
SUB = 8
NEG_FILL = -1e30
BF = jnp.bfloat16
F32 = jnp.float32

NN = (((1,), (0,)), ((), ()))
NT = (((1,), (1,)), ((), ()))
TN = (((0,), (0,)), ((), ()))


def mm(a, b, dims):
    return lax.dot_general(a, b, dims, preferred_element_type=F32)


def shift(v, axis, step, size):
    return lax.ppermute(v, axis, [(i, (i + step) % size) for i in range(size)])


def add2(a, b):
    return (a.astype(F32) + b.astype(F32)).astype(BF)


def grant(mib):
    return pltpu.CompilerParams(vmem_limit_bytes=mib * 1024 * 1024)


def vmem():
    return pl.BlockSpec(memory_space=pltpu.VMEM)


def smem():
    return pl.BlockSpec(memory_space=pltpu.SMEM)


def main_kernel(
    start_ref, mine_ref, other_ref, wk_ref, wv_ref, q_ref, g_ref, slot_ref,
    att_ref, dq_ref, bg_ref, lat_ref, keep_ref, give_ref,
    k_ref, v_ref, acc_ref,
):
    vis = mine_ref.shape[1]
    rows = 2 * mine_ref.shape[0] * SUB
    width = mine_ref.shape[3]
    cols = wk_ref.shape[1]
    heads = cols // DH
    chunk = WIN * rows

    @pl.loop(0, vis // WIN)
    def _(i):
        mine = mine_ref[:, pl.ds(i * WIN, WIN)].astype(F32)
        other = other_ref[:, pl.ds(i * WIN, WIN)].astype(F32)
        parts = []
        for s in range(WIN):
            parts.append(mine[:, s].reshape(rows // 2, width))
            parts.append(other[:, s].reshape(rows // 2, width))
        x = jnp.concatenate(parts, axis=0).astype(BF)
        at = pl.ds(pl.multiple_of(i * chunk, chunk), chunk)
        lat_ref[at, :] = x
        k_ref[at, :] = mm(x, wk_ref[...], NN).astype(BF)
        v_ref[at, :] = mm(x, wv_ref[...], NN).astype(BF)
        acc_ref[at, :] = jnp.zeros((chunk, 2 * cols), F32)

    span = WIN * GAP
    scale = DH ** (-0.5)

    @pl.loop(0, q_ref.shape[0] // span)
    def _(w):
        first = start_ref[w]
        at = pl.ds(pl.multiple_of(first * rows, rows), chunk)
        tok = pl.ds(pl.multiple_of(w * span, span), span)
        slot = slot_ref[w]
        key_slot = first + lax.broadcasted_iota(jnp.int32, (chunk, span), 0) // rows
        match = key_slot == slot
        for h in range(heads):
            c = slice(h * DH, (h + 1) * DH)
            q = q_ref[tok, c]
            g = g_ref[tok, c]
            k = k_ref[at, c]
            v = v_ref[at, c]
            s = jnp.where(match, mm(k, q, NT) * scale, NEG_FILL)
            e = jnp.where(match, jnp.exp(s - jnp.max(s, axis=0, keepdims=True)), 0.0)
            total = jnp.sum(e, axis=0, keepdims=True)
            p = e / jnp.where(total > 0.0, total, 1.0)
            pb = p.astype(BF)
            att_ref[tok, c] = mm(pb, v, TN).astype(BF)
            dp = mm(v, g, NT)
            inner = jnp.sum(p * dp, axis=0, keepdims=True)
            ds = (p * (dp - inner) * scale).astype(BF)
            dq_ref[tok, c] = mm(ds, k, TN).astype(BF)
            acc_ref[at, c] += mm(ds, q, NN)
            acc_ref[at, slice(cols + h * DH, cols + (h + 1) * DH)] += mm(pb, g, NN)

    @pl.loop(0, vis // WIN)
    def _(i):
        at = pl.ds(pl.multiple_of(i * chunk, chunk), chunk)
        grad = acc_ref[at, :].astype(BF)
        bg_ref[at, :] = grad
        out = mm(grad[:, :cols], wk_ref[...], NT) + mm(grad[:, cols:], wv_ref[...], NT)
        for s in range(WIN):
            piece = out[s * rows:(s + 1) * rows].reshape(rows // SUB, SUB, width).astype(BF)
            keep_ref[:, i * WIN + s] = piece[:rows // SUB // 2]
            give_ref[:, i * WIN + s] = piece[rows // SUB // 2:]


def weight_kernel(y_ref, lat_ref, bg_ref, own_ref, next_ref, fa_ref, fb_ref, prev_ref, t_ref, sum_ref):
    nz, part, cols = own_ref.shape
    ny = lat_ref.shape[1] // (nz * part)
    half = t_ref.shape[0]
    step = 256
    zh = nz // 2
    me = y_ref[0]
    for j in range(lat_ref.shape[1] // half):
        t_ref[...] = lat_ref[:, j * half:(j + 1) * half].T

        @pl.loop(0, cols // step)
        def _(n):
            at = pl.ds(pl.multiple_of(n * step, step), step)
            sum_ref[j * half:(j + 1) * half, at] = mm(t_ref[...], bg_ref[:, at], NN)

    def block(z, rel):
        there = lax.rem(me + rel, ny)
        return sum_ref[pl.ds(pl.multiple_of((z * ny + there) * part, SUB), part), :].astype(BF)

    for z in range(nz):
        own_ref[z] = block(z, 0)
        next_ref[z] = block(z, 1)
        prev_ref[z] = block(z, 3)
        if z < zh:
            fa_ref[z] = block(z, 2)
        else:
            fb_ref[z - zh] = block(z, 2)


def collect_kernel(sent_ref, got_ref, out_ref):
    out_ref[...] = jnp.zeros_like(out_ref)

    @pl.loop(0, got_ref.shape[0])
    def _(e):
        image = sent_ref[e]

        @pl.when(image >= 0)
        def _():
            out_ref[image] += got_ref[e].astype(F32)


def local(queries, latents, key_weight, value_weight, visible, outbound, token_slot, grad_out):
    seq = ("z", "y")
    head = ("x", "core")
    nz, ny, nx = (lax.axis_size(a) for a in ("z", "y", "x"))
    tokens, cols = queries.shape
    images, lat_rows, width = latents.shape
    vis = visible.shape[1]
    sent = outbound[0].reshape(-1)
    places = visible[0]
    slots_total = sent.shape[0]
    row_groups = lat_rows // SUB
    part = width // (nz * ny)

    me = lax.axis_index(head)
    pick = jnp.maximum(sent, 0) * row_groups + me
    send = latents.reshape(images * row_groups, SUB, width)[pick]
    got = lax.all_to_all(send, seq, split_axis=0, concat_axis=0, tiled=True)
    own = got[jnp.maximum(places, 0)]

    left = shift(own, "x", 1, nx)
    right = shift(own, "x", -1, nx)
    half = vis // 2
    far_a = shift(left[:half], "x", 1, nx)
    far_b = shift(right[half:], "x", -1, nx)
    mine = jnp.concatenate([own, left, right, far_a, far_b], axis=0).reshape(nx, vis, SUB, width)
    other = shift(mine, "core", 1, 2)

    span = WIN * GAP
    windows = tokens // span
    slot_rows = token_slot.reshape(windows, 1, span)
    start = jnp.minimum(jnp.maximum(slot_rows[:, 0, 0], 0), vis - WIN)
    keys = vis * lat_rows
    att, dq, bg, lat_all, keep, give = pl.pallas_call(
        main_kernel,
        name="main",
        out_shape=(
            jax.ShapeDtypeStruct((tokens, cols), BF),
            jax.ShapeDtypeStruct((tokens, cols), BF),
            jax.ShapeDtypeStruct((keys, 2 * cols), BF),
            jax.ShapeDtypeStruct((keys, width), BF),
            jax.ShapeDtypeStruct((nx, vis, SUB, width), BF),
            jax.ShapeDtypeStruct((nx, vis, SUB, width), BF),
        ),
        in_specs=[smem()] + [vmem()] * 7,
        out_specs=tuple([vmem()] * 6),
        scratch_shapes=[
            pltpu.VMEM((keys, cols), BF),
            pltpu.VMEM((keys, cols), BF),
            pltpu.VMEM((keys, 2 * cols), F32),
        ],
        compiler_params=grant(32),
        cost_estimate=pl.CostEstimate(
            flops=8 * keys * width * cols + 16 * keys * span * cols,
            bytes_accessed=16 * 1024 * 1024,
            transcendentals=tokens * 4 * 256,
        ),
    )(start, mine, other, key_weight, value_weight, queries, grad_out, slot_rows)

    swapped = shift(give, "core", 1, 2)

    y_here = lax.axis_index("y")
    zh = nz // 2
    full = jax.ShapeDtypeStruct((nz, part, 2 * cols), BF)
    split = jax.ShapeDtypeStruct((zh, part, 2 * cols), BF)
    gw_own, gw_next, gw_fa, gw_fb, gw_prev = pl.pallas_call(
        weight_kernel,
        name="weights",
        out_shape=(full, full, split, split, full),
        in_specs=[smem(), vmem(), vmem()],
        out_specs=tuple([vmem()] * 5),
        scratch_shapes=[pltpu.VMEM((width // 2, keys), BF), pltpu.VMEM((width, 2 * cols), F32)],
        compiler_params=grant(24),
        cost_estimate=pl.CostEstimate(
            flops=4 * keys * width * cols, bytes_accessed=8 * 1024 * 1024, transcendentals=0
        ),
    )(y_here.reshape(1).astype(jnp.int32), lat_all, bg)

    swapped, gw_fa, gw_fb = lax.optimization_barrier((swapped, gw_fa, gw_fb))
    gw_up = shift(gw_fa, "y", 1, ny)
    gw_down = shift(gw_fb, "y", -1, ny)

    up = shift(add2(keep[3, :half], swapped[3, :half]), "x", 1, nx)
    down = shift(add2(keep[3, half:], swapped[3, half:]), "x", -1, nx)
    to_right = (keep[2].astype(F32) + swapped[2].astype(F32)
                + jnp.concatenate([up, jnp.zeros_like(up)], axis=0).astype(F32)).astype(BF)
    to_left = (keep[1].astype(F32) + swapped[1].astype(F32)
               + jnp.concatenate([jnp.zeros_like(down), down], axis=0).astype(F32)).astype(BF)
    from_left = shift(to_right, "x", 1, nx)
    from_right = shift(to_left, "x", -1, nx)
    dl_mine = (
        keep[0].astype(F32) + swapped[0].astype(F32) + from_left.astype(F32) + from_right.astype(F32)
    ).astype(BF)

    gw_next = (gw_next.astype(F32)
               + jnp.concatenate([gw_up, jnp.zeros_like(gw_up)], axis=0).astype(F32)).astype(BF)
    gw_prev = (gw_prev.astype(F32)
               + jnp.concatenate([jnp.zeros_like(gw_down), gw_down], axis=0).astype(F32)).astype(BF)
    gw_l = shift(gw_next, "y", 1, ny)
    gw_r = shift(gw_prev, "y", -1, ny)
    gw_y = (gw_own.astype(F32) + gw_l.astype(F32) + gw_r.astype(F32)).astype(BF)

    hits = places[None, :] == jnp.arange(slots_total, dtype=jnp.int32)[:, None]
    back = dl_mine[jnp.argmax(hits, axis=1)]
    returned = lax.all_to_all(back, seq, split_axis=0, concat_axis=0, tiled=True)

    z_here = lax.axis_index("z")
    weights = lax.dynamic_index_in_dim(gw_y, z_here, 0, False).astype(F32)
    for step in (1, -1, 2, -2, 3, -3, 4):
        piece = lax.dynamic_index_in_dim(gw_y, lax.rem(z_here + step + nz, nz), 0, False)
        weights = weights + shift(piece, "z", step, nz).astype(F32)

    grad_latents = pl.pallas_call(
        collect_kernel,
        name="collect",
        out_shape=jax.ShapeDtypeStruct((images, SUB, width), F32),
        in_specs=[smem(), vmem()],
        out_specs=vmem(),
        compiler_params=grant(8),
    )(sent, returned)
    return att, dq, grad_latents, weights[:, :cols], weights[:, cols:]


def solution(mesh):
    sizes = mesh.shape
    nz, ny, nx, core = 8, 4, 4, 2
    assert (sizes["seq"], sizes["head"]) == (nz * ny, nx * core)
    grid = Mesh(mesh.devices.reshape(nz, ny, nx, core), ("z", "y", "x", "core"))
    seq = ("z", "y")
    head = ("x", "core")
    in_specs = (
        P(seq, head),
        P(seq, None, None),
        P(None, head),
        P(None, head),
        P(seq, None),
        P(seq, None, None),
        P(seq),
        P(seq, head),
    )
    out_specs = (
        P(seq, head),
        P(seq, head),
        P(seq, head, None),
        P(seq, head),
        P(seq, head),
    )
    return jax.shard_map(local, mesh=grid, in_specs=in_specs, out_specs=out_specs, check_vma=False)
```

```python
import jax
import jax.numpy as jnp
from jax import lax
from jax.experimental import pallas as pl
from jax.experimental.pallas import tpu as pltpu
from jax.sharding import Mesh
from jax.sharding import PartitionSpec as P

DH = 128
GAP = 32
WIN = 4
SUB = 8
OFFSETS = (0, 3, 1, 2)
NEG_FILL = -1e30
BF = jnp.bfloat16
F32 = jnp.float32

NN = (((1,), (0,)), ((), ()))
NT = (((1,), (1,)), ((), ()))
TN = (((0,), (0,)), ((), ()))


def mm(a, b, dims):
    return lax.dot_general(a, b, dims, preferred_element_type=F32)


def shift(v, axis, step, size):
    return lax.ppermute(v, axis, [(i, (i + step) % size) for i in range(size)])


def add2(a, b):
    return (a.astype(F32) + b.astype(F32)).astype(BF)


def grant(mib):
    return pltpu.CompilerParams(vmem_limit_bytes=mib * 1024 * 1024)


def vmem():
    return pl.BlockSpec(memory_space=pltpu.VMEM)


def smem():
    return pl.BlockSpec(memory_space=pltpu.SMEM)


def spread_kernel(sent_ref, me_ref, lat_ref, out_ref):
    @pl.loop(0, out_ref.shape[0], unroll=4)
    def _(e):
        out_ref[e] = lat_ref[jnp.maximum(sent_ref[e], 0)]


def main_kernel(
    start_ref, pos_ref, mine_ref, other_ref, wk_ref, wv_ref, q_ref, g_ref, slot_ref,
    att_ref, dq_ref, keep_ref, give_ref, own_ref, next_ref, fa_ref, fb_ref, prev_ref,
    lat_ref, k_ref, v_ref, acc_ref, bg_ref, t_ref, sum_ref,
):
    vis = mine_ref.shape[1]
    rows = 2 * mine_ref.shape[0] * SUB
    width = mine_ref.shape[3]
    cols = wk_ref.shape[1]
    heads = cols // DH
    chunk = WIN * rows
    nx = mine_ref.shape[0]
    my_x = pos_ref[0]
    my_y = pos_ref[1]

    @pl.loop(0, vis // WIN)
    def _(i):
        mine = mine_ref[:, pl.ds(i * WIN, WIN)].astype(F32)
        other = other_ref[:, pl.ds(i * WIN, WIN)].astype(F32)
        parts = []
        for s in range(WIN):
            parts.append(mine[:, s].reshape(rows // 2, width))
            parts.append(other[:, s].reshape(rows // 2, width))
        x = jnp.concatenate(parts, axis=0).astype(BF)
        at = pl.ds(pl.multiple_of(i * chunk, chunk), chunk)
        lat_ref[at, :] = x
        k_ref[at, :] = mm(x, wk_ref[...], NN).astype(BF)
        v_ref[at, :] = mm(x, wv_ref[...], NN).astype(BF)
        acc_ref[at, :] = jnp.zeros((chunk, 2 * cols), F32)

    span = WIN * GAP
    scale = DH ** (-0.5)

    @pl.loop(0, q_ref.shape[0] // span)
    def _(w):
        first = start_ref[w]
        at = pl.ds(pl.multiple_of(first * rows, rows), chunk)
        tok = pl.ds(pl.multiple_of(w * span, span), span)
        slot = slot_ref[w]
        key_slot = first + lax.broadcasted_iota(jnp.int32, (chunk, span), 0) // rows
        match = key_slot == slot
        for h in range(heads):
            c = slice(h * DH, (h + 1) * DH)
            q = q_ref[tok, c]
            g = g_ref[tok, c]
            k = k_ref[at, c]
            v = v_ref[at, c]
            s = jnp.where(match, mm(k, q, NT) * scale, NEG_FILL)
            e = jnp.where(match, jnp.exp(s - jnp.max(s, axis=0, keepdims=True)), 0.0)
            total = jnp.sum(e, axis=0, keepdims=True)
            p = e / jnp.where(total > 0.0, total, 1.0)
            pb = p.astype(BF)
            att_ref[tok, c] = mm(pb, v, TN).astype(BF)
            dp = mm(v, g, NT)
            inner = jnp.sum(p * dp, axis=0, keepdims=True)
            ds = (p * (dp - inner) * scale).astype(BF)
            dq_ref[tok, c] = mm(ds, k, TN).astype(BF)
            acc_ref[at, c] += mm(ds, q, NN)
            acc_ref[at, slice(cols + h * DH, cols + (h + 1) * DH)] += mm(pb, g, NN)

    @pl.loop(0, vis // WIN)
    def _(i):
        at = pl.ds(pl.multiple_of(i * chunk, chunk), chunk)
        grad = acc_ref[at, :].astype(BF)
        bg_ref[at, :] = grad
        out = mm(grad[:, :cols], wk_ref[...], NT) + mm(grad[:, cols:], wv_ref[...], NT)
        for s in range(WIN):
            piece = out[s * rows:(s + 1) * rows].reshape(rows // SUB, SUB, width).astype(BF)
            for r, off in enumerate(OFFSETS):
                there = lax.rem(my_x + off, nx)
                keep_ref[there, i * WIN + s] = piece[r]
                give_ref[there, i * WIN + s] = piece[nx + r]

    nz, part, _ = own_ref.shape
    ny = width // (nz * part)
    half = t_ref.shape[0]
    step = 256
    zh = nz // 2
    for j in range(width // half):
        t_ref[...] = lat_ref[:, j * half:(j + 1) * half].T

        @pl.loop(0, 2 * cols // step)
        def _(n):
            at = pl.ds(pl.multiple_of(n * step, step), step)
            sum_ref[j * half:(j + 1) * half, at] = mm(t_ref[...], bg_ref[:, at], NN)

    def block(z, rel):
        there = lax.rem(my_y + rel, ny)
        return sum_ref[pl.ds(pl.multiple_of((z * ny + there) * part, SUB), part), :].astype(BF)

    for z in range(nz):
        own_ref[z] = block(z, 0)
        next_ref[z] = block(z, 1)
        prev_ref[z] = block(z, 3)
        if z < zh:
            fa_ref[z] = block(z, 2)
        else:
            fb_ref[z - zh] = block(z, 2)


def pack_kernel(place_ref, got_ref, out_ref):
    total = got_ref[0].astype(F32)
    for r in range(1, got_ref.shape[0]):
        total = total + got_ref[r].astype(F32)
    total = total.astype(BF)
    for v in range(total.shape[0]):
        place = place_ref[v]

        @pl.when(place >= 0)
        def _():
            out_ref[place] = total[v]


def collect_kernel(sent_ref, got_ref, out_ref):
    out_ref[...] = jnp.zeros_like(out_ref)

    @pl.loop(0, got_ref.shape[0])
    def _(e):
        image = sent_ref[e]

        @pl.when(image >= 0)
        def _():
            out_ref[image] += got_ref[e].astype(F32)


def local(queries, latents, key_weight, value_weight, visible, outbound, token_slot, grad_out):
    seq = ("z", "y")
    head = ("x", "core")
    nz, ny, nx = (lax.axis_size(a) for a in ("z", "y", "x"))
    tokens, cols = queries.shape
    images, lat_rows, width = latents.shape
    vis = visible.shape[1]
    sent = outbound[0].reshape(-1)
    places = visible[0]
    slots_total = sent.shape[0]
    part = width // (nz * ny)

    me = lax.axis_index(head).reshape(1).astype(jnp.int32)
    send = pl.pallas_call(
        spread_kernel,
        name="spread",
        grid_spec=pltpu.PrefetchScalarGridSpec(
            num_scalar_prefetch=2,
            grid=(1,),
            in_specs=[pl.BlockSpec((images, SUB, width), lambda i, a, b: (0, b[0], 0))],
            out_specs=pl.BlockSpec((slots_total, SUB, width), lambda i, a, b: (0, 0, 0)),
        ),
        out_shape=jax.ShapeDtypeStruct((slots_total, SUB, width), BF),
        compiler_params=grant(8),
    )(sent, me, latents)
    got = lax.all_to_all(send, seq, split_axis=0, concat_axis=0, tiled=True)
    own = got[jnp.maximum(places, 0)]

    left = shift(own, "x", 1, nx)
    right = shift(own, "x", -1, nx)
    half = vis // 2
    far_a = shift(left[:half], "x", 1, nx)
    far_b = shift(right[half:], "x", -1, nx)
    mine = jnp.concatenate([own, left, right, far_a, far_b], axis=0).reshape(nx, vis, SUB, width)
    other = shift(mine, "core", 1, 2)

    span = WIN * GAP
    windows = tokens // span
    slot_rows = token_slot.reshape(windows, 1, span)
    start = jnp.minimum(jnp.maximum(slot_rows[:, 0, 0], 0), vis - WIN)
    keys = vis * lat_rows
    zh = nz // 2
    here = jnp.stack([lax.axis_index("x"), lax.axis_index("y")]).astype(jnp.int32)
    tokens_out = jax.ShapeDtypeStruct((tokens, cols), BF)
    rows_out = jax.ShapeDtypeStruct((nx, vis, SUB, width), BF)
    full = jax.ShapeDtypeStruct((nz, part, 2 * cols), BF)
    split = jax.ShapeDtypeStruct((zh, part, 2 * cols), BF)
    att, dq, keep, give, gw_own, gw_next, gw_fa, gw_fb, gw_prev = pl.pallas_call(
        main_kernel,
        name="main",
        out_shape=(tokens_out, tokens_out, rows_out, rows_out, full, full, split, split, full),
        in_specs=[smem(), smem()] + [vmem()] * 7,
        out_specs=tuple([vmem()] * 9),
        scratch_shapes=[
            pltpu.VMEM((keys, width), BF),
            pltpu.VMEM((keys, cols), BF),
            pltpu.VMEM((keys, cols), BF),
            pltpu.VMEM((keys, 2 * cols), F32),
            pltpu.VMEM((keys, 2 * cols), BF),
            pltpu.VMEM((width // 2, keys), BF),
            pltpu.VMEM((width, 2 * cols), F32),
        ],
        compiler_params=grant(26),
        cost_estimate=pl.CostEstimate(
            flops=12 * keys * width * cols + 16 * keys * span * cols,
            bytes_accessed=16 * 1024 * 1024,
            transcendentals=tokens * 4 * 256,
        ),
    )(start, here, mine, other, key_weight, value_weight, queries, grad_out, slot_rows)

    swapped = shift(give, "core", 1, 2)
    gw_up = shift(gw_fa, "y", 1, ny)
    gw_down = shift(gw_fb, "y", -1, ny)
    crossed = lax.all_to_all(add2(keep, swapped), "x", split_axis=0, concat_axis=0, tiled=True)

    gw_next = (gw_next.astype(F32)
               + jnp.concatenate([gw_up, jnp.zeros_like(gw_up)], axis=0).astype(F32)).astype(BF)
    gw_prev = (gw_prev.astype(F32)
               + jnp.concatenate([jnp.zeros_like(gw_down), gw_down], axis=0).astype(F32)).astype(BF)
    gw_l = shift(gw_next, "y", 1, ny)
    gw_r = shift(gw_prev, "y", -1, ny)
    gw_y = (gw_own.astype(F32) + gw_l.astype(F32) + gw_r.astype(F32)).astype(BF)

    back = pl.pallas_call(
        pack_kernel,
        name="pack",
        out_shape=jax.ShapeDtypeStruct((slots_total, SUB, width), BF),
        in_specs=[smem(), vmem()],
        out_specs=vmem(),
        compiler_params=grant(8),
    )(places, crossed)
    returned = lax.all_to_all(back, seq, split_axis=0, concat_axis=0, tiled=True)

    z_here = lax.axis_index("z")
    weights = lax.dynamic_index_in_dim(gw_y, z_here, 0, False).astype(F32)
    arrived = []
    for step in (4, 3, -3, 2, -2, 1, -1):
        piece = lax.dynamic_index_in_dim(gw_y, lax.rem(z_here + step + nz, nz), 0, False)
        arrived.append(shift(piece, "z", step, nz))

    grad_latents = pl.pallas_call(
        collect_kernel,
        name="collect",
        out_shape=jax.ShapeDtypeStruct((images, SUB, width), F32),
        in_specs=[smem(), vmem()],
        out_specs=vmem(),
        compiler_params=grant(8),
    )(sent, returned)
    arrived, grad_latents = lax.optimization_barrier((arrived, grad_latents))
    for piece in arrived:
        weights = weights + piece.astype(F32)
    return att, dq, grad_latents, weights[:, :cols], weights[:, cols:]


def solution(mesh):
    sizes = mesh.shape
    nz, ny, nx, core = 8, 4, 4, 2
    assert (sizes["seq"], sizes["head"]) == (nz * ny, nx * core)
    grid = Mesh(mesh.devices.reshape(nz, ny, nx, core), ("z", "y", "x", "core"))
    seq = ("z", "y")
    head = ("x", "core")
    in_specs = (
        P(seq, head),
        P(seq, None, None),
        P(None, head),
        P(None, head),
        P(seq, None),
        P(seq, None, None),
        P(seq),
        P(seq, head),
    )
    out_specs = (
        P(seq, head),
        P(seq, head),
        P(seq, head, None),
        P(seq, head),
        P(seq, head),
    )
    return jax.shard_map(local, mesh=grid, in_specs=in_specs, out_specs=out_specs, check_vma=False)
```

```python
import jax
import jax.numpy as jnp
from jax import lax
from jax.experimental import pallas as pl
from jax.experimental.pallas import tpu as pltpu
from jax.sharding import Mesh
from jax.sharding import PartitionSpec as P

DH = 128
GAP = 32
WIN = 4
SUB = 8
OFFSETS = (0, 3, 1, 2)
MAIN_MIB = 36
WEIGHT_MIB = 24
SHELF = 16384
NEG_FILL = -1e30
BF = jnp.bfloat16
F32 = jnp.float32

NN = (((1,), (0,)), ((), ()))
NT = (((1,), (1,)), ((), ()))
TN = (((0,), (0,)), ((), ()))


def mm(a, b, dims):
    return lax.dot_general(a, b, dims, preferred_element_type=F32)


def shift(v, axis, step, size):
    return lax.ppermute(v, axis, [(i, (i + step) % size) for i in range(size)])


def add2(a, b):
    return (a.astype(F32) + b.astype(F32)).astype(BF)


def grant(mib):
    return pltpu.CompilerParams(vmem_limit_bytes=mib * 1024 * 1024)


def vmem():
    return pl.BlockSpec(memory_space=pltpu.VMEM)


def anywhere():
    return pl.BlockSpec(memory_space=pl.ANY)


def far():
    return pl.BlockSpec(memory_space=pltpu.HBM)


def smem():
    return pl.BlockSpec(memory_space=pltpu.SMEM)


def spread_kernel(sent_ref, me_ref, lat_ref, out_ref):
    @pl.loop(0, out_ref.shape[0], unroll=4)
    def _(e):
        out_ref[e] = lat_ref[jnp.maximum(sent_ref[e], 0)]


def main_kernel(
    start_ref, pos_ref, mine_any, other_any, wk_any, wv_any, q_any, g_any, slot_ref,
    att_ref, dq_ref, keep_ref, give_ref, shelf_any,
    mine_ref, other_ref, wk_ref, wv_ref, q_ref, g_ref,
    lat_ref, k_ref, v_ref, acc_ref, bg_ref, in_sem, mine_sem, other_sem, lat_sem, bg_sem,
):
    nx, vis = mine_ref.shape[:2]
    rows = 2 * nx * SUB
    width = mine_ref.shape[3]
    cols = wk_ref.shape[1]
    heads = cols // DH
    chunk = WIN * rows
    chunks = vis // WIN
    my_x = pos_ref[0]

    def part_in(src, dst, sem, i):
        at = pl.ds(i * WIN, WIN)
        return pltpu.make_async_copy(src.at[:, at], dst.at[:, at], sem.at[i])

    def part_out(src, base, sem, i):
        at = pl.ds(pl.multiple_of(i * chunk, chunk), chunk)
        to = pl.ds(pl.multiple_of(base + i * chunk, chunk), chunk)
        return pltpu.make_async_copy(src.at[at], shelf_any.at[to, pl.ds(0, src.shape[1])], sem.at[i])

    whole = [
        pltpu.make_async_copy(src, dst, in_sem.at[n])
        for n, (src, dst) in enumerate(
            ((wk_any, wk_ref), (wv_any, wv_ref), (q_any, q_ref), (g_any, g_ref))
        )
    ]
    whole[0].start()
    part_in(mine_any, mine_ref, mine_sem, 0).start()
    part_in(other_any, other_ref, other_sem, 0).start()
    whole[1].start()
    for n in range(1, chunks):
        part_in(mine_any, mine_ref, mine_sem, n).start()
        part_in(other_any, other_ref, other_sem, n).start()
    whole[2].start()
    whole[3].start()
    acc_ref[...] = jnp.zeros_like(acc_ref)
    whole[0].wait()
    whole[1].wait()

    @pl.loop(0, chunks)
    def _(i):
        part_in(mine_any, mine_ref, mine_sem, i).wait()
        part_in(other_any, other_ref, other_sem, i).wait()
        mine = mine_ref[:, pl.ds(i * WIN, WIN)].astype(F32)
        other = other_ref[:, pl.ds(i * WIN, WIN)].astype(F32)
        parts = []
        for s in range(WIN):
            parts.append(mine[:, s].reshape(rows // 2, width))
            parts.append(other[:, s].reshape(rows // 2, width))
        x = jnp.concatenate(parts, axis=0).astype(BF)
        at = pl.ds(pl.multiple_of(i * chunk, chunk), chunk)
        lat_ref[at, :] = x
        k_ref[at, :] = mm(x, wk_ref[...], NN).astype(BF)
        v_ref[at, :] = mm(x, wv_ref[...], NN).astype(BF)
        part_out(lat_ref, 0, lat_sem, i).start()

    whole[2].wait()
    whole[3].wait()
    span = WIN * GAP
    scale = DH ** (-0.5)

    @pl.loop(0, q_ref.shape[0] // span)
    def _(w):
        first = start_ref[w]
        at = pl.ds(pl.multiple_of(first * rows, rows), chunk)
        tok = pl.ds(pl.multiple_of(w * span, span), span)
        slot = slot_ref[w]
        key_slot = first + lax.broadcasted_iota(jnp.int32, (chunk, span), 0) // rows
        match = key_slot == slot
        for h in range(heads):
            c = slice(h * DH, (h + 1) * DH)
            q = q_ref[tok, c]
            g = g_ref[tok, c]
            k = k_ref[at, c]
            v = v_ref[at, c]
            s = jnp.where(match, mm(k, q, NT) * scale, NEG_FILL)
            e = jnp.where(match, jnp.exp(s - jnp.max(s, axis=0, keepdims=True)), 0.0)
            total = jnp.sum(e, axis=0, keepdims=True)
            p = e / jnp.where(total > 0.0, total, 1.0)
            pb = p.astype(BF)
            att_ref[tok, c] = mm(pb, v, TN).astype(BF)
            dp = mm(v, g, NT)
            inner = jnp.sum(p * dp, axis=0, keepdims=True)
            ds = (p * (dp - inner) * scale).astype(BF)
            dq_ref[tok, c] = mm(ds, k, TN).astype(BF)
            acc_ref[at, c] += mm(ds, q, NN)
            acc_ref[at, slice(cols + h * DH, cols + (h + 1) * DH)] += mm(pb, g, NN)

    @pl.loop(0, chunks)
    def _(i):
        at = pl.ds(pl.multiple_of(i * chunk, chunk), chunk)
        grad = acc_ref[at, :].astype(BF)
        bg_ref[at, :] = grad
        part_out(bg_ref, vis * rows, bg_sem, i).start()
        out = mm(grad[:, :cols], wk_ref[...], NT) + mm(grad[:, cols:], wv_ref[...], NT)
        for s in range(WIN):
            piece = out[s * rows:(s + 1) * rows].reshape(rows // SUB, SUB, width).astype(BF)
            for r, off in enumerate(OFFSETS):
                there = lax.rem(my_x + off, nx)
                keep_ref[there, i * WIN + s] = piece[r]
                give_ref[there, i * WIN + s] = piece[nx + r]

    for n in range(chunks):
        part_out(lat_ref, 0, lat_sem, n).wait()
        part_out(bg_ref, vis * rows, bg_sem, n).wait()


def weight_kernel(
    y_ref, shelf_any, own_ref, next_ref, fa_ref, fb_ref, prev_ref,
    lat_ref, bg_ref, t_ref, sum_ref, lat_sem, bg_sem,
):
    nz, part, cols = own_ref.shape
    halves, keys, half = lat_ref.shape
    ny = halves * half // (nz * part)
    my_y = y_ref[0]
    step = 256
    zh = nz // 2
    loads = [
        pltpu.make_async_copy(
            shelf_any.at[pl.ds(0, keys), pl.ds(j * half, half)], lat_ref.at[j], lat_sem.at[j]
        )
        for j in range(halves)
    ]
    rest = pltpu.make_async_copy(shelf_any.at[pl.ds(keys, keys), pl.ds(0, cols)], bg_ref, bg_sem)
    loads[0].start()
    rest.start()
    for load in loads[1:]:
        load.start()
    for j in range(halves):
        loads[j].wait()
        t_ref[...] = lat_ref[j].T
        if j == 0:
            rest.wait()

        @pl.loop(0, cols // step)
        def _(n):
            at = pl.ds(pl.multiple_of(n * step, step), step)
            sum_ref[j * half:(j + 1) * half, at] = mm(t_ref[...], bg_ref[:, at], NN)

    def block(z, rel):
        there = lax.rem(my_y + rel, ny)
        return sum_ref[pl.ds(pl.multiple_of((z * ny + there) * part, SUB), part), :].astype(BF)

    for z in range(nz):
        own_ref[z] = block(z, 0)
        next_ref[z] = block(z, 1)
        prev_ref[z] = block(z, 3)
        if z < zh:
            fa_ref[z] = block(z, 2)
        else:
            fb_ref[z - zh] = block(z, 2)


def pack_kernel(place_ref, got_ref, out_ref):
    total = got_ref[0].astype(F32)
    for r in range(1, got_ref.shape[0]):
        total = total + got_ref[r].astype(F32)
    total = total.astype(BF)
    for v in range(total.shape[0]):
        place = place_ref[v]

        @pl.when(place >= 0)
        def _():
            out_ref[place] = total[v]


def collect_kernel(sent_ref, got_ref, out_ref):
    out_ref[...] = jnp.zeros_like(out_ref)

    @pl.loop(0, got_ref.shape[0])
    def _(e):
        image = sent_ref[e]

        @pl.when(image >= 0)
        def _():
            out_ref[image] += got_ref[e].astype(F32)


def local(queries, latents, key_weight, value_weight, visible, outbound, token_slot, grad_out):
    seq = ("z", "y")
    head = ("x", "core")
    nz, ny, nx = (lax.axis_size(a) for a in ("z", "y", "x"))
    tokens, cols = queries.shape
    images, lat_rows, width = latents.shape
    vis = visible.shape[1]
    sent = outbound[0].reshape(-1)
    places = visible[0]
    slots_total = sent.shape[0]
    part = width // (nz * ny)

    me = lax.axis_index(head).reshape(1).astype(jnp.int32)
    send = pl.pallas_call(
        spread_kernel,
        name="spread",
        grid_spec=pltpu.PrefetchScalarGridSpec(
            num_scalar_prefetch=2,
            grid=(1,),
            in_specs=[pl.BlockSpec((images, SUB, width), lambda i, a, b: (0, b[0], 0))],
            out_specs=pl.BlockSpec((slots_total, SUB, width), lambda i, a, b: (0, 0, 0)),
        ),
        out_shape=jax.ShapeDtypeStruct((slots_total, SUB, width), BF),
        compiler_params=grant(8),
    )(sent, me, latents)
    got = lax.all_to_all(send, seq, split_axis=0, concat_axis=0, tiled=True)
    own = got[jnp.maximum(places, 0)]

    left = shift(own, "x", 1, nx)
    right = shift(own, "x", -1, nx)
    half = vis // 2
    far_a = shift(left[:half], "x", 1, nx)
    far_b = shift(right[half:], "x", -1, nx)
    mine = jnp.concatenate([own, left, right, far_a, far_b], axis=0).reshape(nx, vis, SUB, width)
    other = shift(mine, "core", 1, 2)

    span = WIN * GAP
    windows = tokens // span
    slot_rows = token_slot.reshape(windows, 1, span)
    start = jnp.minimum(jnp.maximum(slot_rows[:, 0, 0], 0), vis - WIN)
    keys = vis * lat_rows
    zh = nz // 2
    x_here = lax.axis_index("x").reshape(1).astype(jnp.int32)
    y_here = lax.axis_index("y").reshape(1).astype(jnp.int32)
    tokens_out = jax.ShapeDtypeStruct((tokens, cols), BF)
    rows_out = jax.ShapeDtypeStruct((nx, vis, SUB, width), BF)
    full = jax.ShapeDtypeStruct((nz, part, 2 * cols), BF)
    split = jax.ShapeDtypeStruct((zh, part, 2 * cols), BF)
    chunks = vis // WIN
    att, dq, keep, give, shelf = pl.pallas_call(
        main_kernel,
        name="main",
        out_shape=(
            tokens_out, tokens_out, rows_out, rows_out,
            jax.ShapeDtypeStruct((SHELF, width), BF),
        ),
        in_specs=[smem(), smem()] + [anywhere()] * 2 + [far()] * 4 + [vmem()],
        out_specs=(vmem(), vmem(), vmem(), vmem(), far()),
        scratch_shapes=[
            pltpu.VMEM((nx, vis, SUB, width), BF),
            pltpu.VMEM((nx, vis, SUB, width), BF),
            pltpu.VMEM((width, cols), BF),
            pltpu.VMEM((width, cols), BF),
            pltpu.VMEM((tokens, cols), BF),
            pltpu.VMEM((tokens, cols), BF),
            pltpu.VMEM((keys, width), BF),
            pltpu.VMEM((keys, cols), BF),
            pltpu.VMEM((keys, cols), BF),
            pltpu.VMEM((keys, 2 * cols), F32),
            pltpu.VMEM((keys, 2 * cols), BF),
            pltpu.SemaphoreType.DMA((4,)),
            pltpu.SemaphoreType.DMA((chunks,)),
            pltpu.SemaphoreType.DMA((chunks,)),
            pltpu.SemaphoreType.DMA((chunks,)),
            pltpu.SemaphoreType.DMA((chunks,)),
        ],
        compiler_params=grant(MAIN_MIB),
        cost_estimate=pl.CostEstimate(
            flops=8 * keys * width * cols + 16 * keys * span * cols,
            bytes_accessed=16 * 1024 * 1024,
            transcendentals=tokens * 4 * 256,
        ),
    )(start, x_here, mine, other, key_weight, value_weight, queries, grad_out, slot_rows)

    swapped = shift(give, "core", 1, 2)
    crossed = lax.all_to_all(add2(keep, swapped), "x", split_axis=0, concat_axis=0, tiled=True)
    gw_own, gw_next, gw_fa, gw_fb, gw_prev = pl.pallas_call(
        weight_kernel,
        name="weights",
        out_shape=(full, full, split, split, full),
        in_specs=[smem(), far()],
        out_specs=tuple([vmem()] * 5),
        scratch_shapes=[
            pltpu.VMEM((2, keys, width // 2), BF),
            pltpu.VMEM((keys, 2 * cols), BF),
            pltpu.VMEM((width // 2, keys), BF),
            pltpu.VMEM((width, 2 * cols), F32),
            pltpu.SemaphoreType.DMA((2,)),
            pltpu.SemaphoreType.DMA,
        ],
        compiler_params=grant(WEIGHT_MIB),
        cost_estimate=pl.CostEstimate(
            flops=4 * keys * width * cols, bytes_accessed=8 * 1024 * 1024, transcendentals=0
        ),
    )(y_here, shelf)
    gw_up = shift(gw_fa, "y", 1, ny)
    gw_down = shift(gw_fb, "y", -1, ny)

    gw_next = (gw_next.astype(F32)
               + jnp.concatenate([gw_up, jnp.zeros_like(gw_up)], axis=0).astype(F32)).astype(BF)
    gw_prev = (gw_prev.astype(F32)
               + jnp.concatenate([jnp.zeros_like(gw_down), gw_down], axis=0).astype(F32)).astype(BF)
    gw_l = shift(gw_next, "y", 1, ny)
    gw_r = shift(gw_prev, "y", -1, ny)
    gw_y = (gw_own.astype(F32) + gw_l.astype(F32) + gw_r.astype(F32)).astype(BF)

    back = pl.pallas_call(
        pack_kernel,
        name="pack",
        out_shape=jax.ShapeDtypeStruct((slots_total, SUB, width), BF),
        in_specs=[smem(), vmem()],
        out_specs=vmem(),
        compiler_params=grant(8),
    )(places, crossed)
    returned = lax.all_to_all(back, seq, split_axis=0, concat_axis=0, tiled=True)

    z_here = lax.axis_index("z")
    weights = lax.dynamic_index_in_dim(gw_y, z_here, 0, False).astype(F32)
    arrived = []
    for step in (4, 3, -3, 2, -2, 1, -1):
        piece = lax.dynamic_index_in_dim(gw_y, lax.rem(z_here + step + nz, nz), 0, False)
        arrived.append(shift(piece, "z", step, nz))

    grad_latents = pl.pallas_call(
        collect_kernel,
        name="collect",
        out_shape=jax.ShapeDtypeStruct((images, SUB, width), F32),
        in_specs=[smem(), vmem()],
        out_specs=vmem(),
        compiler_params=grant(8),
    )(sent, returned)
    arrived, grad_latents = lax.optimization_barrier((arrived, grad_latents))
    for piece in arrived:
        weights = weights + piece.astype(F32)
    return att, dq, grad_latents, weights[:, :cols], weights[:, cols:]


def solution(mesh):
    sizes = mesh.shape
    nz, ny, nx, core = 8, 4, 4, 2
    assert (sizes["seq"], sizes["head"]) == (nz * ny, nx * core)
    grid = Mesh(mesh.devices.reshape(nz, ny, nx, core), ("z", "y", "x", "core"))
    seq = ("z", "y")
    head = ("x", "core")
    in_specs = (
        P(seq, head),
        P(seq, None, None),
        P(None, head),
        P(None, head),
        P(seq, None),
        P(seq, None, None),
        P(seq),
        P(seq, head),
    )
    out_specs = (
        P(seq, head),
        P(seq, head),
        P(seq, head, None),
        P(seq, head),
        P(seq, head),
    )
    return jax.shard_map(local, mesh=grid, in_specs=in_specs, out_specs=out_specs, check_vma=False)
```

```python
import functools

import jax
import jax.numpy as jnp
from jax import lax
from jax.experimental import pallas as pl
from jax.experimental.pallas import tpu as pltpu
from jax.sharding import Mesh
from jax.sharding import PartitionSpec as P

DH = 128
GAP = 32
WIN = 4
SUB = 8
MAIN_MIB = 36
WEIGHT_MIB = 24
SHELF = 16384
NEG_FILL = -1e30
BF = jnp.bfloat16
F32 = jnp.float32

NN = (((1,), (0,)), ((), ()))
NT = (((1,), (1,)), ((), ()))
TN = (((0,), (0,)), ((), ()))


def mm(a, b, dims):
    return lax.dot_general(a, b, dims, preferred_element_type=F32)


def shift(v, axis, step, size):
    return lax.ppermute(v, axis, [(i, (i + step) % size) for i in range(size)])


def add2(a, b):
    return (a.astype(F32) + b.astype(F32)).astype(BF)


def grant(mib):
    return pltpu.CompilerParams(vmem_limit_bytes=mib * 1024 * 1024)


def vmem():
    return pl.BlockSpec(memory_space=pltpu.VMEM)


def anywhere():
    return pl.BlockSpec(memory_space=pl.ANY)


def far():
    return pl.BlockSpec(memory_space=pltpu.HBM)


def smem():
    return pl.BlockSpec(memory_space=pltpu.SMEM)


def spread_kernel(sent_ref, me_ref, lat_any, out_ref, lat_ref, sem):
    at = pl.ds(pl.multiple_of(me_ref[0] * SUB, SUB), SUB)
    load = pltpu.make_async_copy(lat_any.at[:, at], lat_ref, sem)
    load.start()
    load.wait()

    @pl.loop(0, out_ref.shape[0], unroll=4)
    def _(e):
        out_ref[e] = lat_ref[jnp.maximum(sent_ref[e], 0)]


def main_kernel(
    start_ref, mine_any, other_any, wk_any, wv_any, q_any, g_any, slot_ref,
    att_ref, dq_ref, keep_ref, give_ref, shelf_any,
    mine_ref, other_ref, wk_ref, wv_ref, q_ref, g_ref,
    lat_ref, k_ref, v_ref, acc_ref, bg_ref, in_sem, mine_sem, other_sem, lat_sem, bg_sem,
):
    nx, vis = mine_ref.shape[:2]
    rows = 2 * nx * SUB
    width = mine_ref.shape[3]
    cols = wk_ref.shape[1]
    heads = cols // DH
    chunk = WIN * rows
    chunks = vis // WIN

    def part_in(src, dst, sem, i):
        at = pl.ds(i * WIN, WIN)
        return pltpu.make_async_copy(src.at[:, at], dst.at[:, at], sem.at[i])

    def part_out(src, base, sem, i):
        at = pl.ds(pl.multiple_of(i * chunk, chunk), chunk)
        to = pl.ds(pl.multiple_of(base + i * chunk, chunk), chunk)
        return pltpu.make_async_copy(src.at[at], shelf_any.at[to, pl.ds(0, src.shape[1])], sem.at[i])

    whole = [
        pltpu.make_async_copy(src, dst, in_sem.at[n])
        for n, (src, dst) in enumerate(
            ((wk_any, wk_ref), (wv_any, wv_ref), (q_any, q_ref), (g_any, g_ref))
        )
    ]
    whole[0].start()
    part_in(mine_any, mine_ref, mine_sem, 0).start()
    part_in(other_any, other_ref, other_sem, 0).start()
    whole[1].start()
    for n in range(1, chunks):
        part_in(mine_any, mine_ref, mine_sem, n).start()
        part_in(other_any, other_ref, other_sem, n).start()
    whole[2].start()
    whole[3].start()
    acc_ref[...] = jnp.zeros_like(acc_ref)
    whole[0].wait()
    whole[1].wait()

    @pl.loop(0, chunks)
    def _(i):
        part_in(mine_any, mine_ref, mine_sem, i).wait()
        part_in(other_any, other_ref, other_sem, i).wait()
        mine = mine_ref[:, pl.ds(i * WIN, WIN)].astype(F32)
        other = other_ref[:, pl.ds(i * WIN, WIN)].astype(F32)
        parts = []
        for s in range(WIN):
            parts.append(mine[:, s].reshape(rows // 2, width))
            parts.append(other[:, s].reshape(rows // 2, width))
        x = jnp.concatenate(parts, axis=0).astype(BF)
        at = pl.ds(pl.multiple_of(i * chunk, chunk), chunk)
        lat_ref[at, :] = x
        k_ref[at, :] = mm(x, wk_ref[...], NN).astype(BF)
        v_ref[at, :] = mm(x, wv_ref[...], NN).astype(BF)
        part_out(lat_ref, 0, lat_sem, i).start()

    whole[2].wait()
    whole[3].wait()
    span = WIN * GAP
    scale = DH ** (-0.5)

    @pl.loop(0, q_ref.shape[0] // span)
    def _(w):
        first = start_ref[w]
        at = pl.ds(pl.multiple_of(first * rows, rows), chunk)
        tok = pl.ds(pl.multiple_of(w * span, span), span)
        slot = slot_ref[w]
        key_slot = first + lax.broadcasted_iota(jnp.int32, (chunk, span), 0) // rows
        match = key_slot == slot
        for h in range(heads):
            c = slice(h * DH, (h + 1) * DH)
            q = q_ref[tok, c]
            g = g_ref[tok, c]
            k = k_ref[at, c]
            v = v_ref[at, c]
            s = jnp.where(match, mm(k, q, NT) * scale, NEG_FILL)
            e = jnp.where(match, jnp.exp(s - jnp.max(s, axis=0, keepdims=True)), 0.0)
            total = jnp.sum(e, axis=0, keepdims=True)
            p = e / jnp.where(total > 0.0, total, 1.0)
            pb = p.astype(BF)
            att_ref[tok, c] = mm(pb, v, TN).astype(BF)
            dp = mm(v, g, NT)
            inner = jnp.sum(p * dp, axis=0, keepdims=True)
            ds = (p * (dp - inner) * scale).astype(BF)
            dq_ref[tok, c] = mm(ds, k, TN).astype(BF)
            acc_ref[at, c] += mm(ds, q, NN)
            acc_ref[at, slice(cols + h * DH, cols + (h + 1) * DH)] += mm(pb, g, NN)

    @pl.loop(0, chunks)
    def _(i):
        at = pl.ds(pl.multiple_of(i * chunk, chunk), chunk)
        grad = acc_ref[at, :].astype(BF)
        bg_ref[at, :] = grad
        part_out(bg_ref, vis * rows, bg_sem, i).start()
        out = mm(grad[:, :cols], wk_ref[...], NT) + mm(grad[:, cols:], wv_ref[...], NT)
        for s in range(WIN):
            piece = out[s * rows:(s + 1) * rows].reshape(rows // SUB, SUB, width).astype(BF)
            keep_ref[:, i * WIN + s] = piece[:nx]
            give_ref[:, i * WIN + s] = piece[nx:]

    for n in range(chunks):
        part_out(lat_ref, 0, lat_sem, n).wait()
        part_out(bg_ref, vis * rows, bg_sem, n).wait()


def weight_kernel(
    base, y_ref, shelf_any, own_ref, next_ref, far_ref, prev_ref,
    lat_ref, bg_ref, t_ref, sum_ref, lat_sem, bg_sem,
):
    nz, part, cols = own_ref.shape
    keys, half = lat_ref.shape
    ny = half // (nz * part)
    my_y = y_ref[0]
    step = 256
    load = pltpu.make_async_copy(shelf_any.at[pl.ds(0, keys), pl.ds(base, half)], lat_ref, lat_sem)
    rest = pltpu.make_async_copy(shelf_any.at[pl.ds(keys, keys), pl.ds(0, cols)], bg_ref, bg_sem)
    load.start()
    rest.start()
    load.wait()
    t_ref[...] = lat_ref[...].T
    rest.wait()

    @pl.loop(0, cols // step)
    def _(n):
        at = pl.ds(pl.multiple_of(n * step, step), step)
        sum_ref[:, at] = mm(t_ref[...], bg_ref[:, at], NN)

    for rel, out_ref in enumerate((own_ref, next_ref, far_ref, prev_ref)):
        there = lax.rem(my_y + rel, ny)
        for z in range(nz):
            rows = pl.ds(pl.multiple_of((z * ny + there) * part, SUB), part)
            out_ref[z] = sum_ref[rows, :].astype(BF)


def pack_kernel(place_ref, own_ref, left_ref, right_ref, far_ref, out_ref):
    total = own_ref[...].astype(F32)
    for got_ref in (left_ref, right_ref, far_ref):
        total = total + got_ref[...].astype(F32)
    total = total.astype(BF)
    for v in range(total.shape[0]):
        place = place_ref[v]

        @pl.when(place >= 0)
        def _():
            out_ref[place] = total[v]


def collect_kernel(sent_ref, got_ref, out_ref):
    out_ref[...] = jnp.zeros_like(out_ref)

    @pl.loop(0, got_ref.shape[0])
    def _(e):
        image = sent_ref[e]

        @pl.when(image >= 0)
        def _():
            out_ref[image] += got_ref[e].astype(F32)


def local(queries, latents, key_weight, value_weight, visible, outbound, token_slot, grad_out):
    seq = ("z", "y")
    head = ("x", "core")
    nz, ny, nx = (lax.axis_size(a) for a in ("z", "y", "x"))
    tokens, cols = queries.shape
    images, lat_rows, width = latents.shape
    vis = visible.shape[1]
    sent = outbound[0].reshape(-1)
    places = visible[0]
    slots_total = sent.shape[0]
    part = width // (nz * ny)

    me = lax.axis_index(head).reshape(1).astype(jnp.int32)
    send = pl.pallas_call(
        spread_kernel,
        name="spread",
        in_specs=[smem(), smem(), far()],
        out_specs=vmem(),
        scratch_shapes=[pltpu.VMEM((images, SUB, width), BF), pltpu.SemaphoreType.DMA],
        out_shape=jax.ShapeDtypeStruct((slots_total, SUB, width), BF),
        compiler_params=grant(8),
    )(sent, me, latents)
    got = lax.all_to_all(send, seq, split_axis=0, concat_axis=0, tiled=True)
    own = got[jnp.maximum(places, 0)]

    left = shift(own, "x", 1, nx)
    right = shift(own, "x", -1, nx)
    half = vis // 2
    far_a = shift(left[:half], "x", 1, nx)
    far_b = shift(right[half:], "x", -1, nx)
    mine = jnp.concatenate([own, left, right, far_a, far_b], axis=0).reshape(nx, vis, SUB, width)
    other = shift(mine, "core", 1, 2)

    span = WIN * GAP
    windows = tokens // span
    slot_rows = token_slot.reshape(windows, 1, span)
    start = jnp.minimum(jnp.maximum(slot_rows[:, 0, 0], 0), vis - WIN)
    keys = vis * lat_rows
    zh = nz // 2
    y_here = lax.axis_index("y").reshape(1).astype(jnp.int32)
    tokens_out = jax.ShapeDtypeStruct((tokens, cols), BF)
    rows_out = jax.ShapeDtypeStruct((nx, vis, SUB, width), BF)
    split = jax.ShapeDtypeStruct((zh, part, 2 * cols), BF)
    chunks = vis // WIN
    att, dq, keep, give, shelf = pl.pallas_call(
        main_kernel,
        name="main",
        out_shape=(
            tokens_out, tokens_out, rows_out, rows_out,
            jax.ShapeDtypeStruct((SHELF, width), BF),
        ),
        in_specs=[smem()] + [anywhere()] * 2 + [far()] * 4 + [vmem()],
        out_specs=(vmem(), vmem(), vmem(), vmem(), far()),
        scratch_shapes=[
            pltpu.VMEM((nx, vis, SUB, width), BF),
            pltpu.VMEM((nx, vis, SUB, width), BF),
            pltpu.VMEM((width, cols), BF),
            pltpu.VMEM((width, cols), BF),
            pltpu.VMEM((tokens, cols), BF),
            pltpu.VMEM((tokens, cols), BF),
            pltpu.VMEM((keys, width), BF),
            pltpu.VMEM((keys, cols), BF),
            pltpu.VMEM((keys, cols), BF),
            pltpu.VMEM((keys, 2 * cols), F32),
            pltpu.VMEM((keys, 2 * cols), BF),
            pltpu.SemaphoreType.DMA((4,)),
            pltpu.SemaphoreType.DMA((chunks,)),
            pltpu.SemaphoreType.DMA((chunks,)),
            pltpu.SemaphoreType.DMA((chunks,)),
            pltpu.SemaphoreType.DMA((chunks,)),
        ],
        compiler_params=grant(MAIN_MIB),
        cost_estimate=pl.CostEstimate(
            flops=8 * keys * width * cols + 16 * keys * span * cols,
            bytes_accessed=16 * 1024 * 1024,
            transcendentals=tokens * 4 * 256,
        ),
    )(start, mine, other, key_weight, value_weight, queries, grad_out, slot_rows)

    swapped = shift(give, "core", 1, 2)

    def heavy(n):
        return pl.pallas_call(
            functools.partial(weight_kernel, n * (width // 2)),
            out_shape=(split,) * 4,
            in_specs=[smem(), far()],
            out_specs=(vmem(),) * 4,
            scratch_shapes=[
                pltpu.VMEM((keys, width // 2), BF),
                pltpu.VMEM((keys, 2 * cols), BF),
                pltpu.VMEM((width // 2, keys), BF),
                pltpu.VMEM((width // 2, 2 * cols), F32),
                pltpu.SemaphoreType.DMA,
                pltpu.SemaphoreType.DMA,
            ],
            compiler_params=grant(WEIGHT_MIB),
            cost_estimate=pl.CostEstimate(
                flops=2 * keys * width * cols, bytes_accessed=6 * 1024 * 1024, transcendentals=0
            ),
        )(y_here, shelf)

    own_a, next_a, far_a, prev_a = heavy(0)
    own_b, next_b, far_b, prev_b = heavy(1)
    summed = [add2(keep[r], swapped[r]) for r in range(nx)]
    from_far = shift(summed[3], "x", 2, nx)
    from_left = shift(summed[2], "x", 1, nx)
    from_right = shift(summed[1], "x", -1, nx)

    gw_up = shift(far_a, "y", 1, ny)
    gw_down = shift(far_b, "y", -1, ny)
    gw_next = jnp.concatenate([add2(next_a, gw_up), next_b], axis=0)
    gw_prev = jnp.concatenate([prev_a, add2(prev_b, gw_down)], axis=0)
    gw_l = shift(gw_next, "y", 1, ny)
    gw_r = shift(gw_prev, "y", -1, ny)
    gw_own = jnp.concatenate([own_a, own_b], axis=0)
    gw_y = (gw_own.astype(F32) + gw_l.astype(F32) + gw_r.astype(F32)).astype(BF)

    back = pl.pallas_call(
        pack_kernel,
        name="pack",
        out_shape=jax.ShapeDtypeStruct((slots_total, SUB, width), BF),
        in_specs=[smem()] + [vmem()] * 4,
        out_specs=vmem(),
        compiler_params=grant(8),
    )(places, summed[0], from_left, from_right, from_far)
    returned = lax.all_to_all(back, seq, split_axis=0, concat_axis=0, tiled=True)

    z_here = lax.axis_index("z")
    weights = lax.dynamic_index_in_dim(gw_y, z_here, 0, False).astype(F32)
    arrived = []
    for step in (4, 3, -3, 2, -2, 1, -1):
        piece = lax.dynamic_index_in_dim(gw_y, lax.rem(z_here + step + nz, nz), 0, False)
        arrived.append(shift(piece, "z", step, nz))

    grad_latents = pl.pallas_call(
        collect_kernel,
        name="collect",
        out_shape=jax.ShapeDtypeStruct((images, SUB, width), F32),
        in_specs=[smem(), vmem()],
        out_specs=vmem(),
        compiler_params=grant(8),
    )(sent, returned)
    arrived, grad_latents = lax.optimization_barrier((arrived, grad_latents))
    for piece in arrived:
        weights = weights + piece.astype(F32)
    return att, dq, grad_latents, weights[:, :cols], weights[:, cols:]


def solution(mesh):
    sizes = mesh.shape
    nz, ny, nx, core = 8, 4, 4, 2
    assert (sizes["seq"], sizes["head"]) == (nz * ny, nx * core)
    grid = Mesh(mesh.devices.reshape(nz, ny, nx, core), ("z", "y", "x", "core"))
    seq = ("z", "y")
    head = ("x", "core")
    in_specs = (
        P(seq, head),
        P(seq, None, None),
        P(None, head),
        P(None, head),
        P(seq, None),
        P(seq, None, None),
        P(seq),
        P(seq, head),
    )
    out_specs = (
        P(seq, head),
        P(seq, head),
        P(seq, head, None),
        P(seq, head),
        P(seq, head),
    )
    return jax.shard_map(local, mesh=grid, in_specs=in_specs, out_specs=out_specs, check_vma=False)
```

```python
import functools

import jax
import jax.numpy as jnp
from jax import lax
from jax.experimental import pallas as pl
from jax.experimental.pallas import tpu as pltpu
from jax.sharding import Mesh
from jax.sharding import PartitionSpec as P

DH = 128
GAP = 32
WIN = 4
SUB = 8
MAIN_MIB = 36
WEIGHT_MIB = 24
SHELF = 16384
NEG_FILL = -1e30
BF = jnp.bfloat16
F32 = jnp.float32

NN = (((1,), (0,)), ((), ()))
NT = (((1,), (1,)), ((), ()))
TN = (((0,), (0,)), ((), ()))


def mm(a, b, dims):
    return lax.dot_general(a, b, dims, preferred_element_type=F32)


def shift(v, axis, step, size):
    return lax.ppermute(v, axis, [(i, (i + step) % size) for i in range(size)])


def add2(a, b):
    return (a.astype(F32) + b.astype(F32)).astype(BF)


def grant(mib):
    return pltpu.CompilerParams(vmem_limit_bytes=mib * 1024 * 1024)


def vmem():
    return pl.BlockSpec(memory_space=pltpu.VMEM)


def anywhere():
    return pl.BlockSpec(memory_space=pl.ANY)


def far():
    return pl.BlockSpec(memory_space=pltpu.HBM)


def smem():
    return pl.BlockSpec(memory_space=pltpu.SMEM)


def spread_kernel(sent_ref, me_ref, lat_any, out_ref, lat_ref, sem):
    at = pl.ds(pl.multiple_of(me_ref[0] * SUB, SUB), SUB)
    load = pltpu.make_async_copy(lat_any.at[:, at], lat_ref, sem)
    load.start()
    load.wait()

    @pl.loop(0, out_ref.shape[0], unroll=4)
    def _(e):
        out_ref[e] = lat_ref[jnp.maximum(sent_ref[e], 0)]


def main_kernel(
    start_ref, mine_any, other_any, wk_any, wv_any, q_any, g_any, slot_ref,
    att_ref, dq_ref, keep_ref, give_ref, shelf_any,
    mine_ref, other_ref, wk_ref, wv_ref, q_ref, g_ref,
    lat_ref, k_ref, v_ref, acc_ref, bg_ref, in_sem, mine_sem, other_sem, lat_sem, bg_sem,
):
    nx, vis = mine_ref.shape[:2]
    rows = 2 * nx * SUB
    width = mine_ref.shape[3]
    cols = wk_ref.shape[1]
    heads = cols // DH
    chunk = WIN * rows
    chunks = vis // WIN

    def part_in(src, dst, sem, i):
        at = pl.ds(i * WIN, WIN)
        return pltpu.make_async_copy(src.at[:, at], dst.at[:, at], sem.at[i])

    def part_out(src, base, sem, i):
        at = pl.ds(pl.multiple_of(i * chunk, chunk), chunk)
        to = pl.ds(pl.multiple_of(base + i * chunk, chunk), chunk)
        return pltpu.make_async_copy(src.at[at], shelf_any.at[to, pl.ds(0, src.shape[1])], sem.at[i])

    whole = [
        pltpu.make_async_copy(src, dst, in_sem.at[n])
        for n, (src, dst) in enumerate(
            ((wk_any, wk_ref), (wv_any, wv_ref), (q_any, q_ref), (g_any, g_ref))
        )
    ]
    whole[0].start()
    part_in(mine_any, mine_ref, mine_sem, 0).start()
    part_in(other_any, other_ref, other_sem, 0).start()
    whole[1].start()
    for n in range(1, chunks):
        part_in(mine_any, mine_ref, mine_sem, n).start()
        part_in(other_any, other_ref, other_sem, n).start()
    whole[2].start()
    whole[3].start()
    acc_ref[...] = jnp.zeros_like(acc_ref)
    whole[0].wait()
    whole[1].wait()

    @pl.loop(0, chunks)
    def _(i):
        part_in(mine_any, mine_ref, mine_sem, i).wait()
        part_in(other_any, other_ref, other_sem, i).wait()
        mine = mine_ref[:, pl.ds(i * WIN, WIN)].astype(F32)
        other = other_ref[:, pl.ds(i * WIN, WIN)].astype(F32)
        parts = []
        for s in range(WIN):
            parts.append(mine[:, s].reshape(rows // 2, width))
            parts.append(other[:, s].reshape(rows // 2, width))
        x = jnp.concatenate(parts, axis=0).astype(BF)
        at = pl.ds(pl.multiple_of(i * chunk, chunk), chunk)
        lat_ref[at, :] = x
        k_ref[at, :] = mm(x, wk_ref[...], NN).astype(BF)
        v_ref[at, :] = mm(x, wv_ref[...], NN).astype(BF)
        part_out(lat_ref, 0, lat_sem, i).start()

    whole[2].wait()
    whole[3].wait()
    span = WIN * GAP
    scale = DH ** (-0.5)

    @pl.loop(0, q_ref.shape[0] // span)
    def _(w):
        first = start_ref[w]
        at = pl.ds(pl.multiple_of(first * rows, rows), chunk)
        tok = pl.ds(pl.multiple_of(w * span, span), span)
        slot = slot_ref[w]
        key_slot = first + lax.broadcasted_iota(jnp.int32, (chunk, span), 0) // rows
        match = key_slot == slot
        for h in range(heads):
            c = slice(h * DH, (h + 1) * DH)
            q = q_ref[tok, c]
            g = g_ref[tok, c]
            k = k_ref[at, c]
            v = v_ref[at, c]
            s = jnp.where(match, mm(k, q, NT) * scale, NEG_FILL)
            e = jnp.where(match, jnp.exp(s - jnp.max(s, axis=0, keepdims=True)), 0.0)
            total = jnp.sum(e, axis=0, keepdims=True)
            p = e / jnp.where(total > 0.0, total, 1.0)
            pb = p.astype(BF)
            att_ref[tok, c] = mm(pb, v, TN).astype(BF)
            dp = mm(v, g, NT)
            inner = jnp.sum(p * dp, axis=0, keepdims=True)
            ds = (p * (dp - inner) * scale).astype(BF)
            dq_ref[tok, c] = mm(ds, k, TN).astype(BF)
            acc_ref[at, c] += mm(ds, q, NN)
            acc_ref[at, slice(cols + h * DH, cols + (h + 1) * DH)] += mm(pb, g, NN)

    @pl.loop(0, chunks)
    def _(i):
        at = pl.ds(pl.multiple_of(i * chunk, chunk), chunk)
        grad = acc_ref[at, :].astype(BF)
        bg_ref[at, :] = grad
        part_out(bg_ref, vis * rows, bg_sem, i).start()
        out = mm(grad[:, :cols], wk_ref[...], NT) + mm(grad[:, cols:], wv_ref[...], NT)
        for s in range(WIN):
            piece = out[s * rows:(s + 1) * rows].reshape(rows // SUB, SUB, width).astype(BF)
            keep_ref[:, i * WIN + s] = piece[:nx]
            give_ref[:, i * WIN + s] = piece[nx:]

    for n in range(chunks):
        part_out(lat_ref, 0, lat_sem, n).wait()
        part_out(bg_ref, vis * rows, bg_sem, n).wait()


def weight_kernel(
    base, y_ref, shelf_any, own_ref, next_ref, far_ref, prev_ref,
    lat_ref, bg_ref, t_ref, sum_ref, lat_sem, bg_sem,
):
    nz, part, cols = own_ref.shape
    keys, half = lat_ref.shape
    ny = half // (nz * part)
    my_y = y_ref[0]
    step = 256
    load = pltpu.make_async_copy(shelf_any.at[pl.ds(0, keys), pl.ds(base, half)], lat_ref, lat_sem)
    rest = pltpu.make_async_copy(shelf_any.at[pl.ds(keys, keys), pl.ds(0, cols)], bg_ref, bg_sem)
    load.start()
    rest.start()
    load.wait()
    t_ref[...] = lat_ref[...].T
    rest.wait()

    @pl.loop(0, cols // step)
    def _(n):
        at = pl.ds(pl.multiple_of(n * step, step), step)
        sum_ref[:, at] = mm(t_ref[...], bg_ref[:, at], NN)

    for rel, out_ref in enumerate((own_ref, next_ref, far_ref, prev_ref)):
        there = lax.rem(my_y + rel, ny)
        for z in range(nz):
            rows = pl.ds(pl.multiple_of((z * ny + there) * part, SUB), part)
            out_ref[z] = sum_ref[rows, :].astype(BF)


def pack_kernel(place_ref, own_ref, left_ref, right_ref, far_ref, out_ref):
    total = own_ref[...].astype(F32)
    for got_ref in (left_ref, right_ref, far_ref):
        total = total + got_ref[...].astype(F32)
    total = total.astype(BF)
    for v in range(total.shape[0]):
        place = place_ref[v]

        @pl.when(place >= 0)
        def _():
            out_ref[place] = total[v]


def collect_kernel(sent_ref, got_ref, out_ref):
    out_ref[...] = jnp.zeros_like(out_ref)

    @pl.loop(0, got_ref.shape[0])
    def _(e):
        image = sent_ref[e]

        @pl.when(image >= 0)
        def _():
            out_ref[image] += got_ref[e].astype(F32)


def local(queries, latents, key_weight, value_weight, visible, outbound, token_slot, grad_out):
    seq = ("z", "y")
    head = ("x", "core")
    nz, ny, nx = (lax.axis_size(a) for a in ("z", "y", "x"))
    tokens, cols = queries.shape
    images, lat_rows, width = latents.shape
    vis = visible.shape[1]
    sent = outbound[0].reshape(-1)
    places = visible[0]
    slots_total = sent.shape[0]
    part = width // (nz * ny)

    me = lax.axis_index(head).reshape(1).astype(jnp.int32)
    send = pl.pallas_call(
        spread_kernel,
        name="spread",
        in_specs=[smem(), smem(), far()],
        out_specs=vmem(),
        scratch_shapes=[pltpu.VMEM((images, SUB, width), BF), pltpu.SemaphoreType.DMA],
        out_shape=jax.ShapeDtypeStruct((slots_total, SUB, width), BF),
        compiler_params=grant(8),
    )(sent, me, latents)
    got = lax.all_to_all(send, seq, split_axis=0, concat_axis=0, tiled=True)
    own = got[jnp.maximum(places, 0)]

    left = shift(own, "x", 1, nx)
    right = shift(own, "x", -1, nx)
    half = vis // 2
    far_a = shift(left[:half], "x", 1, nx)
    far_b = shift(right[half:], "x", -1, nx)
    mine = jnp.concatenate([own, left, right, far_a, far_b], axis=0).reshape(nx, vis, SUB, width)
    other = shift(mine, "core", 1, 2)

    span = WIN * GAP
    windows = tokens // span
    slot_rows = token_slot.reshape(windows, 1, span)
    start = jnp.minimum(jnp.maximum(slot_rows[:, 0, 0], 0), vis - WIN)
    keys = vis * lat_rows
    zh = nz // 2
    y_here = lax.axis_index("y").reshape(1).astype(jnp.int32)
    tokens_out = jax.ShapeDtypeStruct((tokens, cols), BF)
    rows_out = jax.ShapeDtypeStruct((nx, vis, SUB, width), BF)
    split = jax.ShapeDtypeStruct((zh, part, 2 * cols), BF)
    chunks = vis // WIN
    att, dq, keep, give, shelf = pl.pallas_call(
        main_kernel,
        name="main",
        out_shape=(
            tokens_out, tokens_out, rows_out, rows_out,
            jax.ShapeDtypeStruct((SHELF, width), BF),
        ),
        in_specs=[smem()] + [anywhere()] * 2 + [far()] * 4 + [vmem()],
        out_specs=(vmem(), vmem(), vmem(), vmem(), far()),
        scratch_shapes=[
            pltpu.VMEM((nx, vis, SUB, width), BF),
            pltpu.VMEM((nx, vis, SUB, width), BF),
            pltpu.VMEM((width, cols), BF),
            pltpu.VMEM((width, cols), BF),
            pltpu.VMEM((tokens, cols), BF),
            pltpu.VMEM((tokens, cols), BF),
            pltpu.VMEM((keys, width), BF),
            pltpu.VMEM((keys, cols), BF),
            pltpu.VMEM((keys, cols), BF),
            pltpu.VMEM((keys, 2 * cols), F32),
            pltpu.VMEM((keys, 2 * cols), BF),
            pltpu.SemaphoreType.DMA((4,)),
            pltpu.SemaphoreType.DMA((chunks,)),
            pltpu.SemaphoreType.DMA((chunks,)),
            pltpu.SemaphoreType.DMA((chunks,)),
            pltpu.SemaphoreType.DMA((chunks,)),
        ],
        compiler_params=grant(MAIN_MIB),
        cost_estimate=pl.CostEstimate(
            flops=8 * keys * width * cols + 16 * keys * span * cols,
            bytes_accessed=16 * 1024 * 1024,
            transcendentals=tokens * 4 * 256,
        ),
    )(start, mine, other, key_weight, value_weight, queries, grad_out, slot_rows)

    swapped = shift(give, "core", 1, 2)

    def heavy(n):
        return pl.pallas_call(
            functools.partial(weight_kernel, n * (width // 2)),
            out_shape=(split,) * 4,
            in_specs=[smem(), far()],
            out_specs=(vmem(),) * 4,
            scratch_shapes=[
                pltpu.VMEM((keys, width // 2), BF),
                pltpu.VMEM((keys, 2 * cols), BF),
                pltpu.VMEM((width // 2, keys), BF),
                pltpu.VMEM((width // 2, 2 * cols), F32),
                pltpu.SemaphoreType.DMA,
                pltpu.SemaphoreType.DMA,
            ],
            compiler_params=grant(WEIGHT_MIB),
            cost_estimate=pl.CostEstimate(
                flops=2 * keys * width * cols, bytes_accessed=6 * 1024 * 1024, transcendentals=0
            ),
        )(y_here, shelf)

    own_a, next_a, far_a, prev_a = heavy(0)
    own_b, next_b, far_b, prev_b = heavy(1)
    summed = [add2(keep[r], swapped[r]) for r in range(nx)]
    from_far = shift(summed[3], "x", 2, nx)
    from_left = shift(summed[2], "x", 1, nx)
    from_right = shift(summed[1], "x", -1, nx)

    gw_up = shift(far_a, "y", 1, ny)
    far_high = shift(far_b, "y", 2, ny)
    prev_low = shift(prev_a, "y", -1, ny)
    next_high = shift(next_b, "y", 1, ny)
    next_low = shift(add2(next_a, gw_up), "y", 1, ny)
    prev_high = shift(prev_b, "y", -1, ny)
    gw_y = jnp.concatenate(
        [
            (own_a.astype(F32) + next_low.astype(F32) + prev_low.astype(F32)).astype(BF),
            (
                own_b.astype(F32) + next_high.astype(F32) + prev_high.astype(F32) + far_high.astype(F32)
            ).astype(BF),
        ],
        axis=0,
    )

    back = pl.pallas_call(
        pack_kernel,
        name="pack",
        out_shape=jax.ShapeDtypeStruct((slots_total, SUB, width), BF),
        in_specs=[smem()] + [vmem()] * 4,
        out_specs=vmem(),
        compiler_params=grant(8),
    )(places, summed[0], from_left, from_right, from_far)
    returned = lax.all_to_all(back, seq, split_axis=0, concat_axis=0, tiled=True)

    z_here = lax.axis_index("z")
    weights = lax.dynamic_index_in_dim(gw_y, z_here, 0, False).astype(F32)
    arrived = []
    for step in (4, 3, -3, 2, -2, 1, -1):
        piece = lax.dynamic_index_in_dim(gw_y, lax.rem(z_here + step + nz, nz), 0, False)
        arrived.append(shift(piece, "z", step, nz))

    grad_latents = pl.pallas_call(
        collect_kernel,
        name="collect",
        out_shape=jax.ShapeDtypeStruct((images, SUB, width), F32),
        in_specs=[smem(), vmem()],
        out_specs=vmem(),
        compiler_params=grant(8),
    )(sent, returned)
    arrived, grad_latents = lax.optimization_barrier((arrived, grad_latents))
    for piece in arrived:
        weights = weights + piece.astype(F32)
    return att, dq, grad_latents, weights[:, :cols], weights[:, cols:]


def solution(mesh):
    sizes = mesh.shape
    nz, ny, nx, core = 8, 4, 4, 2
    assert (sizes["seq"], sizes["head"]) == (nz * ny, nx * core)
    grid = Mesh(mesh.devices.reshape(nz, ny, nx, core), ("z", "y", "x", "core"))
    seq = ("z", "y")
    head = ("x", "core")
    in_specs = (
        P(seq, head),
        P(seq, None, None),
        P(None, head),
        P(None, head),
        P(seq, None),
        P(seq, None, None),
        P(seq),
        P(seq, head),
    )
    out_specs = (
        P(seq, head),
        P(seq, head),
        P(seq, head, None),
        P(seq, head),
        P(seq, head),
    )
    return jax.shard_map(local, mesh=grid, in_specs=in_specs, out_specs=out_specs, check_vma=False)
```

```python
import functools

import jax
import jax.numpy as jnp
from jax import lax
from jax.experimental import pallas as pl
from jax.experimental.pallas import tpu as pltpu
from jax.sharding import Mesh
from jax.sharding import PartitionSpec as P

DH = 128
GAP = 32
WIN = 4
SUB = 8
MAIN_MIB = 36
WEIGHT_MIB = 24
SHELF = 16384
NEG_FILL = -1e30
BF = jnp.bfloat16
F32 = jnp.float32

NN = (((1,), (0,)), ((), ()))
NT = (((1,), (1,)), ((), ()))
TN = (((0,), (0,)), ((), ()))


def mm(a, b, dims):
    return lax.dot_general(a, b, dims, preferred_element_type=F32)


def shift(v, axis, step, size):
    return lax.ppermute(v, axis, [(i, (i + step) % size) for i in range(size)])


def add2(a, b):
    return (a.astype(F32) + b.astype(F32)).astype(BF)


def grant(mib):
    return pltpu.CompilerParams(vmem_limit_bytes=mib * 1024 * 1024)


def vmem():
    return pl.BlockSpec(memory_space=pltpu.VMEM)


def anywhere():
    return pl.BlockSpec(memory_space=pl.ANY)


def far():
    return pl.BlockSpec(memory_space=pltpu.HBM)


def smem():
    return pl.BlockSpec(memory_space=pltpu.SMEM)


def spread_kernel(sent_ref, me_ref, lat_any, out_ref, lat_ref, sem):
    at = pl.ds(pl.multiple_of(me_ref[0] * SUB, SUB), SUB)
    load = pltpu.make_async_copy(lat_any.at[:, at], lat_ref, sem)
    load.start()
    load.wait()

    @pl.loop(0, out_ref.shape[0], unroll=4)
    def _(e):
        out_ref[e] = lat_ref[jnp.maximum(sent_ref[e], 0)]


def main_kernel(
    start_ref, mine_any, other_any, wk_any, wv_any, q_any, g_any, slot_ref,
    att_ref, dq_ref, keep_ref, give_ref, shelf_any,
    mine_ref, other_ref, wk_ref, wv_ref, q_ref, g_ref,
    lat_ref, k_ref, v_ref, acc_ref, bg_ref, in_sem, mine_sem, other_sem, lat_sem, bg_sem,
):
    nx, vis = mine_ref.shape[:2]
    rows = 2 * nx * SUB
    width = mine_ref.shape[3]
    cols = wk_ref.shape[1]
    heads = cols // DH
    chunk = WIN * rows
    chunks = vis // WIN

    def part_in(src, dst, sem, i):
        at = pl.ds(i * WIN, WIN)
        return pltpu.make_async_copy(src.at[:, at], dst.at[:, at], sem.at[i])

    def part_out(src, base, sem, i):
        at = pl.ds(pl.multiple_of(i * chunk, chunk), chunk)
        to = pl.ds(pl.multiple_of(base + i * chunk, chunk), chunk)
        return pltpu.make_async_copy(src.at[at], shelf_any.at[to, pl.ds(0, src.shape[1])], sem.at[i])

    whole = [
        pltpu.make_async_copy(src, dst, in_sem.at[n])
        for n, (src, dst) in enumerate(
            ((wk_any, wk_ref), (wv_any, wv_ref), (q_any, q_ref), (g_any, g_ref))
        )
    ]
    whole[0].start()
    part_in(mine_any, mine_ref, mine_sem, 0).start()
    part_in(other_any, other_ref, other_sem, 0).start()
    whole[1].start()
    for n in range(1, chunks):
        part_in(mine_any, mine_ref, mine_sem, n).start()
        part_in(other_any, other_ref, other_sem, n).start()
    whole[2].start()
    whole[3].start()
    acc_ref[...] = jnp.zeros_like(acc_ref)
    whole[0].wait()
    whole[1].wait()

    @pl.loop(0, chunks)
    def _(i):
        part_in(mine_any, mine_ref, mine_sem, i).wait()
        part_in(other_any, other_ref, other_sem, i).wait()
        mine = mine_ref[:, pl.ds(i * WIN, WIN)].astype(F32)
        other = other_ref[:, pl.ds(i * WIN, WIN)].astype(F32)
        parts = []
        for s in range(WIN):
            parts.append(mine[:, s].reshape(rows // 2, width))
            parts.append(other[:, s].reshape(rows // 2, width))
        x = jnp.concatenate(parts, axis=0).astype(BF)
        at = pl.ds(pl.multiple_of(i * chunk, chunk), chunk)
        lat_ref[at, :] = x
        k_ref[at, :] = mm(x, wk_ref[...], NN).astype(BF)
        v_ref[at, :] = mm(x, wv_ref[...], NN).astype(BF)
        part_out(lat_ref, 0, lat_sem, i).start()

    whole[2].wait()
    whole[3].wait()
    span = WIN * GAP
    scale = DH ** (-0.5)

    @pl.loop(0, q_ref.shape[0] // span)
    def _(w):
        first = start_ref[w]
        at = pl.ds(pl.multiple_of(first * rows, rows), chunk)
        tok = pl.ds(pl.multiple_of(w * span, span), span)
        slot = slot_ref[w]
        key_slot = first + lax.broadcasted_iota(jnp.int32, (chunk, span), 0) // rows
        match = key_slot == slot
        for h in range(heads):
            c = slice(h * DH, (h + 1) * DH)
            q = q_ref[tok, c]
            g = g_ref[tok, c]
            k = k_ref[at, c]
            v = v_ref[at, c]
            s = jnp.where(match, mm(k, q, NT) * scale, NEG_FILL)
            e = jnp.where(match, jnp.exp(s - jnp.max(s, axis=0, keepdims=True)), 0.0)
            total = jnp.sum(e, axis=0, keepdims=True)
            p = e / jnp.where(total > 0.0, total, 1.0)
            pb = p.astype(BF)
            att_ref[tok, c] = mm(pb, v, TN).astype(BF)
            dp = mm(v, g, NT)
            inner = jnp.sum(p * dp, axis=0, keepdims=True)
            ds = (p * (dp - inner) * scale).astype(BF)
            dq_ref[tok, c] = mm(ds, k, TN).astype(BF)
            acc_ref[at, c] += mm(ds, q, NN)
            acc_ref[at, slice(cols + h * DH, cols + (h + 1) * DH)] += mm(pb, g, NN)

    @pl.loop(0, chunks)
    def _(i):
        at = pl.ds(pl.multiple_of(i * chunk, chunk), chunk)
        grad = acc_ref[at, :].astype(BF)
        bg_ref[at, :] = grad
        part_out(bg_ref, vis * rows, bg_sem, i).start()
        out = mm(grad[:, :cols], wk_ref[...], NT) + mm(grad[:, cols:], wv_ref[...], NT)
        for s in range(WIN):
            piece = out[s * rows:(s + 1) * rows].reshape(rows // SUB, SUB, width).astype(BF)
            keep_ref[:, i * WIN + s] = piece[:nx]
            give_ref[:, i * WIN + s] = piece[nx:]

    for n in range(chunks):
        part_out(lat_ref, 0, lat_sem, n).wait()
        part_out(bg_ref, vis * rows, bg_sem, n).wait()


def weight_kernel(
    base, y_ref, shelf_any, *refs,
):
    early_refs = refs[:-10]
    own_ref, next_ref, far_ref, prev_ref, lat_ref, bg_ref, t_ref, sum_ref, lat_sem, bg_sem = refs[-10:]
    nz, part, cols = own_ref.shape
    skip = prev_ref.shape[0] - nz
    keys, half = lat_ref.shape
    ny = half // (nz * part)
    my_y = y_ref[0]
    step = 256
    load = pltpu.make_async_copy(shelf_any.at[pl.ds(0, keys), pl.ds(base, half)], lat_ref, lat_sem)
    rest = pltpu.make_async_copy(shelf_any.at[pl.ds(keys, keys), pl.ds(0, cols)], bg_ref, bg_sem)
    load.start()
    rest.start()
    load.wait()
    t_ref[...] = lat_ref[...].T
    rest.wait()

    @pl.loop(0, cols // step)
    def _(n):
        at = pl.ds(pl.multiple_of(n * step, step), step)
        sum_ref[:, at] = mm(t_ref[...], bg_ref[:, at], NN)

    for rel, out_ref in enumerate((own_ref, next_ref, far_ref, prev_ref)):
        there = lax.rem(my_y + rel, ny)
        for z in range(nz):
            rows = pl.ds(pl.multiple_of((z * ny + there) * part, SUB), part)
            spot = z + skip if out_ref is prev_ref else z
            out_ref[spot] = sum_ref[rows, :].astype(BF)
    for early_ref in early_refs:
        prev_ref[:skip] = early_ref[...]


def pack_kernel(place_ref, own_ref, left_ref, right_ref, far_ref, out_ref):
    total = own_ref[...].astype(F32)
    for got_ref in (left_ref, right_ref, far_ref):
        total = total + got_ref[...].astype(F32)
    total = total.astype(BF)
    for v in range(total.shape[0]):
        place = place_ref[v]

        @pl.when(place >= 0)
        def _():
            out_ref[place] = total[v]


def collect_kernel(sent_ref, got_ref, out_ref, sum_ref):
    images = out_ref.shape[0]
    sum_ref[...] = jnp.zeros_like(sum_ref)

    @pl.loop(0, got_ref.shape[0], unroll=4)
    def _(e):
        image = sent_ref[e]
        at = jnp.where(image >= 0, image, images)
        sum_ref[at] += got_ref[e].astype(F32)

    out_ref[...] = sum_ref[:images]


def local(queries, latents, key_weight, value_weight, visible, outbound, token_slot, grad_out):
    seq = ("z", "y")
    head = ("x", "core")
    nz, ny, nx = (lax.axis_size(a) for a in ("z", "y", "x"))
    tokens, cols = queries.shape
    images, lat_rows, width = latents.shape
    vis = visible.shape[1]
    sent = outbound[0].reshape(-1)
    places = visible[0]
    slots_total = sent.shape[0]
    part = width // (nz * ny)

    me = lax.axis_index(head).reshape(1).astype(jnp.int32)
    send = pl.pallas_call(
        spread_kernel,
        name="spread",
        in_specs=[smem(), smem(), far()],
        out_specs=vmem(),
        scratch_shapes=[pltpu.VMEM((images, SUB, width), BF), pltpu.SemaphoreType.DMA],
        out_shape=jax.ShapeDtypeStruct((slots_total, SUB, width), BF),
        compiler_params=grant(8),
    )(sent, me, latents)
    got = lax.all_to_all(send, seq, split_axis=0, concat_axis=0, tiled=True)
    own = got[jnp.maximum(places, 0)]

    left = shift(own, "x", 1, nx)
    right = shift(own, "x", -1, nx)
    half = vis // 2
    far_a = shift(left[:half], "x", 1, nx)
    far_b = shift(right[half:], "x", -1, nx)
    mine = jnp.concatenate([own, left, right, far_a, far_b], axis=0).reshape(nx, vis, SUB, width)
    other = shift(mine, "core", 1, 2)

    span = WIN * GAP
    windows = tokens // span
    slot_rows = token_slot.reshape(windows, 1, span)
    start = jnp.minimum(jnp.maximum(slot_rows[:, 0, 0], 0), vis - WIN)
    keys = vis * lat_rows
    zh = nz // 2
    y_here = lax.axis_index("y").reshape(1).astype(jnp.int32)
    tokens_out = jax.ShapeDtypeStruct((tokens, cols), BF)
    rows_out = jax.ShapeDtypeStruct((nx, vis, SUB, width), BF)
    split = jax.ShapeDtypeStruct((zh, part, 2 * cols), BF)
    full = jax.ShapeDtypeStruct((nz, part, 2 * cols), BF)
    chunks = vis // WIN
    att, dq, keep, give, shelf = pl.pallas_call(
        main_kernel,
        name="main",
        out_shape=(
            tokens_out, tokens_out, rows_out, rows_out,
            jax.ShapeDtypeStruct((SHELF, width), BF),
        ),
        in_specs=[smem()] + [anywhere()] * 2 + [far()] * 4 + [vmem()],
        out_specs=(vmem(), vmem(), vmem(), vmem(), far()),
        scratch_shapes=[
            pltpu.VMEM((nx, vis, SUB, width), BF),
            pltpu.VMEM((nx, vis, SUB, width), BF),
            pltpu.VMEM((width, cols), BF),
            pltpu.VMEM((width, cols), BF),
            pltpu.VMEM((tokens, cols), BF),
            pltpu.VMEM((tokens, cols), BF),
            pltpu.VMEM((keys, width), BF),
            pltpu.VMEM((keys, cols), BF),
            pltpu.VMEM((keys, cols), BF),
            pltpu.VMEM((keys, 2 * cols), F32),
            pltpu.VMEM((keys, 2 * cols), BF),
            pltpu.SemaphoreType.DMA((4,)),
            pltpu.SemaphoreType.DMA((chunks,)),
            pltpu.SemaphoreType.DMA((chunks,)),
            pltpu.SemaphoreType.DMA((chunks,)),
            pltpu.SemaphoreType.DMA((chunks,)),
        ],
        compiler_params=grant(MAIN_MIB),
        cost_estimate=pl.CostEstimate(
            flops=8 * keys * width * cols + 16 * keys * span * cols,
            bytes_accessed=16 * 1024 * 1024,
            transcendentals=tokens * 4 * 256,
        ),
    )(start, mine, other, key_weight, value_weight, queries, grad_out, slot_rows)

    swapped = shift(give, "core", 1, 2)

    def heavy(n, *early):
        return pl.pallas_call(
            functools.partial(weight_kernel, n * (width // 2)),
            out_shape=(split, split, split, full if early else split),
            in_specs=[smem(), far()] + [vmem()] * len(early),
            out_specs=(vmem(),) * 4,
            scratch_shapes=[
                pltpu.VMEM((keys, width // 2), BF),
                pltpu.VMEM((keys, 2 * cols), BF),
                pltpu.VMEM((width // 2, keys), BF),
                pltpu.VMEM((width // 2, 2 * cols), F32),
                pltpu.SemaphoreType.DMA,
                pltpu.SemaphoreType.DMA,
            ],
            compiler_params=grant(WEIGHT_MIB),
            cost_estimate=pl.CostEstimate(
                flops=2 * keys * width * cols, bytes_accessed=6 * 1024 * 1024, transcendentals=0
            ),
        )(y_here, shelf, *early)

    own_a, next_a, far_a, prev_a = heavy(0)
    own_b, next_b, far_b, prev_all = heavy(1, prev_a)
    summed = [add2(keep[r], swapped[r]) for r in range(nx)]
    from_far = shift(summed[3], "x", 2, nx)
    from_left = shift(summed[2], "x", 1, nx)
    from_right = shift(summed[1], "x", -1, nx)

    relayed = shift(far_a, "y", 1, ny)
    far_high = shift(far_b, "y", 2, ny)
    prev_got = shift(prev_all, "y", -1, ny)
    next_high = shift(next_b, "y", 1, ny)
    next_low = shift(add2(next_a, relayed), "y", 1, ny)
    gw_y = jnp.concatenate(
        [
            (own_a.astype(F32) + next_low.astype(F32) + prev_got[:zh].astype(F32)).astype(BF),
            (
                own_b.astype(F32)
                + next_high.astype(F32)
                + prev_got[zh:].astype(F32)
                + far_high.astype(F32)
            ).astype(BF),
        ],
        axis=0,
    )

    back = pl.pallas_call(
        pack_kernel,
        name="pack",
        out_shape=jax.ShapeDtypeStruct((slots_total, SUB, width), BF),
        in_specs=[smem()] + [vmem()] * 4,
        out_specs=vmem(),
        compiler_params=grant(8),
    )(places, summed[0], from_left, from_right, from_far)
    returned = lax.all_to_all(back, seq, split_axis=0, concat_axis=0, tiled=True)

    z_here = lax.axis_index("z")
    weights = lax.dynamic_index_in_dim(gw_y, z_here, 0, False).astype(F32)
    arrived = []
    for step in (4, 3, -3, 2, -2, 1, -1):
        piece = lax.dynamic_index_in_dim(gw_y, lax.rem(z_here + step + nz, nz), 0, False)
        arrived.append(shift(piece, "z", step, nz))

    grad_latents = pl.pallas_call(
        collect_kernel,
        name="collect",
        out_shape=jax.ShapeDtypeStruct((images, SUB, width), F32),
        in_specs=[smem(), vmem()],
        out_specs=vmem(),
        scratch_shapes=[pltpu.VMEM((images + 1, SUB, width), F32)],
        compiler_params=grant(8),
    )(sent, returned)
    arrived, grad_latents = lax.optimization_barrier((arrived, grad_latents))
    for piece in arrived:
        weights = weights + piece.astype(F32)
    return att, dq, grad_latents, weights[:, :cols], weights[:, cols:]


def solution(mesh):
    sizes = mesh.shape
    nz, ny, nx, core = 8, 4, 4, 2
    assert (sizes["seq"], sizes["head"]) == (nz * ny, nx * core)
    grid = Mesh(mesh.devices.reshape(nz, ny, nx, core), ("z", "y", "x", "core"))
    seq = ("z", "y")
    head = ("x", "core")
    in_specs = (
        P(seq, head),
        P(seq, None, None),
        P(None, head),
        P(None, head),
        P(seq, None),
        P(seq, None, None),
        P(seq),
        P(seq, head),
    )
    out_specs = (
        P(seq, head),
        P(seq, head),
        P(seq, head, None),
        P(seq, head),
        P(seq, head),
    )
    return jax.shard_map(local, mesh=grid, in_specs=in_specs, out_specs=out_specs, check_vma=False)
```
